32 devices in a mesh: rows: 16 (over z, y, core), cols: 2 (over x).
Axes of the slice: x: 2, y: 2, z: 4, core: 2. Of those that a mesh axis runs over, the one named last changes fastest.
Arguments:
- inputs: bfloat16 [96, 64, 640], P('rows', 'cols'), may hold values from -4 to 4
- qkv_weight: bfloat16 [640, 960], replicated, may hold values from -0.25 to 0.25
- out_weight: bfloat16 [320, 640], replicated, may hold values from -0.3125 to 0.3125
- attn_out: bfloat16 [96, 64, 320], P('rows', 'cols'), may hold values from -6 to 6
- log_norm: float32 [5, 96, 64], P(None, 'rows', 'cols'), may hold values from 4 to 6
- cotangent: bfloat16 [96, 64, 640], P('rows', 'cols'), may hold values from -6 to 6
Outputs:
- grad_input: bfloat16 [96, 64, 640], P('rows', 'cols')
- grad_qkv_weight: bfloat16 [640, 960], replicated
- grad_out_weight: bfloat16 [320, 640], replicated
The draws below stay inside these ranges and needn't reach their ends.
All inputs are finite; a program needn't handle non-finite values.
Results may differ from the reference program's by a relative error of at most 0.01.
Values may be sent and summed in bfloat16 or wider, within the bound.
A program may use at most 64 MiB of HBM per device.

```python
import jax
import jax.numpy as jnp
from jax import lax

D = 640
HEADS = 5
HEAD_DIM = 64
RADIUS = 6
INNER = 320
GRID_ROWS = 96
GRID_COLS = 64


def draw_inputs(key, part):
    values = jnp.clip(jax.random.normal(key, (GRID_ROWS, GRID_COLS, D), jnp.float32), -4.0, 4.0)
    return values.astype(jnp.bfloat16)


def levels(rng, extent, pieces, least, high):
    factor_of = 1.0
    for dim, parts in pieces:
        steps = jax.random.uniform(jax.random.fold_in(jax.random.fold_in(rng, 6), dim), (parts,), jnp.float32, least / len(pieces), high / len(pieces))
        factor_of = factor_of * jnp.repeat(jnp.exp(steps), extent[dim] // parts).reshape((-1,) + (1,) * (len(extent) - 1 - dim))
    return factor_of


def normal_values(key, shape, spread, limit, split=(), kind=jnp.bfloat16):
    values = spread * jax.random.normal(key, shape, jnp.float32)
    if split:
        values = values * levels(key, shape, split, -0.22, 0.18)
    return jnp.clip(values, -limit, limit).astype(kind)


def setup_inputs(seed: int = 0) -> dict:
    key_list = jax.random.split(jax.random.key(seed), 7)
    return {
        "inputs": draw_inputs(jax.random.fold_in(key_list[6], 71), 0),
        "qkv_weight": normal_values(key_list[1], (D, 3 * INNER), D ** -0.5, 0.25),
        "out_weight": normal_values(key_list[2], (INNER, D), INNER ** -0.5, 0.3125),
        "attn_out": normal_values(key_list[3], (GRID_ROWS, GRID_COLS, INNER), 1.0, 6.0, ((0, 16), (1, 2))),
        "log_norm": jnp.clip(4.0 + 2.0 * jax.random.uniform(key_list[4], (HEADS, GRID_ROWS, GRID_COLS), jnp.float32) ** levels(key_list[4], (HEADS, GRID_ROWS, GRID_COLS), ((1, 16), (2, 2)), -0.2, 0.2), 4.0, 6.0),
        "cotangent": normal_values(key_list[5], (GRID_ROWS, GRID_COLS, D), 1.0, 6.0, ((0, 16), (1, 2))),
    }


def reference(inputs, qkv_weight, out_weight, attn_out, log_norm, cotangent):
    grid_rows, grid_cols, model_width = inputs.shape
    inner_width = HEADS * HEAD_DIM
    score_scale = HEAD_DIM ** -0.5
    grid_tokens = grid_rows * grid_cols
    flat_in = inputs.reshape(grid_tokens, model_width)
    flat_cot = cotangent.reshape(grid_tokens, model_width)
    flat_att = attn_out.reshape(grid_tokens, inner_width)
    projected = jnp.dot(flat_in, qkv_weight, preferred_element_type=jnp.float32).astype(jnp.bfloat16)
    grad_att = jnp.dot(flat_cot, out_weight.T, preferred_element_type=jnp.float32).astype(jnp.bfloat16)
    grad_wout = jnp.dot(flat_att.T, flat_cot, preferred_element_type=jnp.float32)
    head_shape = (grid_rows, grid_cols, HEADS, HEAD_DIM)
    queries = projected[:, :inner_width].reshape(head_shape).astype(jnp.float32)
    keys_all = projected[:, inner_width:2 * inner_width].reshape(head_shape).astype(jnp.float32)
    values_all = projected[:, 2 * inner_width:].reshape(head_shape).astype(jnp.float32)
    upstream = grad_att.reshape(head_shape).astype(jnp.float32)
    row_delta = jnp.sum(upstream * flat_att.reshape(head_shape).astype(jnp.float32), axis=3)
    own_norm = jnp.transpose(log_norm, (1, 2, 0))
    row_ids = jnp.arange(grid_rows, dtype=jnp.int32).reshape(grid_rows, 1, 1)
    window_side = 2 * RADIUS + 1

    def visit_offset(totals, offset):
        grad_query, grad_key, grad_value = totals
        shift_rows = offset // window_side - RADIUS
        shift_cols = offset % window_side - RADIUS
        key_here = jnp.roll(keys_all, (-shift_rows, -shift_cols), (0, 1))
        value_here = jnp.roll(values_all, (-shift_rows, -shift_cols), (0, 1))
        in_grid = (row_ids + shift_rows >= 0) & (row_ids + shift_rows < grid_rows)
        scores = score_scale * jnp.sum(queries * key_here, axis=3)
        weight = jnp.where(in_grid, jnp.exp(scores - own_norm), 0.0)
        grad_weight = jnp.sum(upstream * value_here, axis=3)
        grad_score = lax.optimization_barrier((weight * (grad_weight - row_delta)).astype(jnp.bfloat16)).astype(jnp.float32)
        weight_low = lax.optimization_barrier(weight.astype(jnp.bfloat16)).astype(jnp.float32)
        grad_query = grad_query + grad_score[..., None] * key_here
        grad_key = grad_key + jnp.roll(grad_score[..., None] * queries, (shift_rows, shift_cols), (0, 1))
        grad_value = grad_value + jnp.roll(weight_low[..., None] * upstream, (shift_rows, shift_cols), (0, 1))
        return (grad_query, grad_key, grad_value), None

    zeros_init = jnp.zeros(head_shape, jnp.float32)
    offsets = jnp.arange(window_side * window_side, dtype=jnp.int32)
    finals, ignored = lax.scan(visit_offset, (zeros_init, zeros_init, zeros_init), offsets)
    grad_query, grad_key, grad_value = finals
    grad_proj = jnp.concatenate([
        (score_scale * grad_query).reshape(grid_tokens, inner_width),
        (score_scale * grad_key).reshape(grid_tokens, inner_width),
        grad_value.reshape(grid_tokens, inner_width)], axis=1).astype(jnp.bfloat16)
    grad_input = jnp.dot(grad_proj, qkv_weight.T, preferred_element_type=jnp.float32).astype(jnp.bfloat16)
    grad_input = grad_input.reshape(grid_rows, grid_cols, model_width)
    grad_factor = grid_tokens ** -0.5
    grad_wqkv = jnp.dot(flat_in.T, grad_proj, preferred_element_type=jnp.float32)
    return grad_input, (grad_wqkv * grad_factor).astype(jnp.bfloat16), (grad_wout * grad_factor).astype(jnp.bfloat16)
```

```python
import functools

import jax
import jax.numpy as jnp
from jax import lax
from jax.experimental import pallas as pl
from jax.experimental.pallas import tpu as pltpu
from jax.sharding import PartitionSpec as P

HEADS = 5
HEAD_DIM = 64
RADIUS = 6


MESH = pl.DeviceIdType.MESH


def reduce_kernel(
    planes, depth, width, factor,
    x_ref, o_ref, recv1, sum1, recv2, sum2, recv3,
    s1, r1, s2, r2, s3, r3, zs, zr, ps, pr, cs, cr,
):
    row, col = lax.axis_index("rows"), lax.axis_index("cols")
    core, lane, z = row % 2, (row // 2) % 2, row // 4
    p = lane * width + col
    partner = (row + 1 - 2 * core, col)

    def plane_peer(k):
        q = (p + k) % planes
        return q, (z * 4 + (q // width) * 2 + core, q % width)

    def z_peer(k):
        q = (z + k) % depth
        return q, (q * 4 + lane * 2 + core, col)

    def send(src, dst, ssem, rsem, device):
        copy = pltpu.make_async_remote_copy(
            src_ref=src, dst_ref=dst, send_sem=ssem, recv_sem=rsem,
            device_id=device, device_id_type=MESH,
        )
        copy.start()
        return copy

    barrier = pltpu.get_barrier_semaphore()
    peers = [partner]
    peers += [plane_peer(k)[1] for k in range(1, planes)]
    peers += [z_peer(k)[1] for k in range(1, depth)]
    for peer in peers:
        pl.semaphore_signal(barrier, inc=1, device_id=peer, device_id_type=MESH)
    pl.semaphore_wait(barrier, len(peers))

    order = list(range(1, planes)) + [0]
    pair, started = {}, []
    for k in order:
        q = (p + k) % planes
        pair[k] = send(x_ref.at[1 - core, q], recv1.at[k], s1.at[k], r1.at[k], partner)
    across = {}
    for k in order:
        q, device = plane_peer(k)
        pair[k].wait_recv()
        total = x_ref[core, q].astype(jnp.float32) + recv1[k].astype(jnp.float32)
        sum1[k] = total.astype(jnp.bfloat16)
        if k:
            across[k] = send(sum1.at[k], recv2.at[k - 1], s2.at[k - 1], r2.at[k - 1], device)
    total = sum1[0].astype(jnp.float32)
    for k in range(1, planes):
        across[k].wait_recv()
        total = total + recv2[k - 1].astype(jnp.float32)
    sum2[...] = total.astype(jnp.bfloat16)
    deep = {}
    for k in range(1, depth):
        q, device = z_peer(k)
        deep[k] = send(sum2.at[q], recv3.at[k - 1], s3.at[k - 1], r3.at[k - 1], device)
    total = sum2[z].astype(jnp.float32)
    for k in range(1, depth):
        deep[k].wait_recv()
        total = total + recv3[k - 1].astype(jnp.float32)
    o_ref[core, p, z] = (total * factor).astype(jnp.bfloat16)

    own = o_ref.at[core, p, z]
    zcopies, pcopies = {}, {}
    for k in range(1, depth):
        zcopies[k] = send(own, own, zs.at[k - 1], zr.at[k - 1], z_peer(k)[1])

    def share(kz, piece):
        for k in range(1, planes):
            pcopies[k, kz] = send(
                piece, piece, ps.at[k - 1, kz], pr.at[k - 1, kz], plane_peer(k)[1]
            )
        started.append(send(piece, piece, cs.at[0, kz], cr.at[0, kz], partner))

    share(0, own)
    for k in range(1, depth):
        zcopies[k].wait_recv()
        share(k, o_ref.at[core, p, (z - k + depth) % depth])
    for kz in range(depth):
        for k in range(1, planes):
            pcopies[k, kz].wait_recv()
            piece = o_ref.at[core, (p - k + planes) % planes, (z - kz + depth) % depth]
            started.append(send(piece, piece, cs.at[k, kz], cr.at[k, kz], partner))
    for copy in started:
        copy.wait_recv()
    for copy in [*started, *pair.values(), *across.values(), *deep.values(),
                 *zcopies.values(), *pcopies.values()]:
        copy.wait_send()


def summed(parts, factor):
    rows = parts.shape[0]
    columns = parts.shape[1]
    count, width = lax.axis_size("rows"), lax.axis_size("cols")
    planes, depth = 2 * width, max(count // 4, 1)
    half = columns // 2
    if count % 4 or rows % (planes * depth * 8) or columns % 256 or depth < 2:
        return (lax.psum(parts, ("rows", "cols")) * factor).astype(jnp.bfloat16)
    high = rows // (planes * depth)
    x = parts.astype(jnp.bfloat16).reshape(planes, depth, high, 2, half).transpose(3, 0, 1, 2, 4)
    low = jnp.bfloat16
    dma = pltpu.SemaphoreType.DMA
    out = pl.pallas_call(
        functools.partial(reduce_kernel, planes, depth, width, factor),
        out_shape=jax.ShapeDtypeStruct((2, planes, depth, high, half), low),
        in_specs=[pl.BlockSpec(memory_space=pltpu.VMEM)],
        out_specs=pl.BlockSpec(memory_space=pltpu.VMEM),
        scratch_shapes=[
            pltpu.VMEM((planes, depth, high, half), low),
            pltpu.VMEM((planes, depth, high, half), low),
            pltpu.VMEM((planes - 1, depth, high, half), low),
            pltpu.VMEM((depth, high, half), low),
            pltpu.VMEM((depth - 1, high, half), low),
            dma((planes,)), dma((planes,)),
            dma((planes - 1,)), dma((planes - 1,)),
            dma((depth - 1,)), dma((depth - 1,)),
            dma((depth - 1,)), dma((depth - 1,)),
            dma((planes - 1, depth)), dma((planes - 1, depth)),
            dma((planes, depth)), dma((planes, depth)),
        ],
        compiler_params=pltpu.CompilerParams(collective_id=0, has_side_effects=True),
        name="weight_sums",
    )(x)
    return out.transpose(1, 2, 3, 0, 4).reshape(rows, columns)


def padded(block, sides, width):
    for axis, dim in sides:
        count = lax.axis_size(axis)
        forward = [(i, i + 1) for i in range(count - 1)]
        forward.append((count - 1, 0))
        backward = [(target, source) for source, target in forward]
        low = lax.ppermute(
            lax.slice_in_dim(block, block.shape[dim] - width, None, axis=dim), axis, forward
        )
        high = lax.ppermute(lax.slice_in_dim(block, 0, width, axis=dim), axis, backward)
        block = jnp.concatenate([low, block, high], axis=dim)
    return block


def window_mask(rows_dev, cols_dev, row_start, grid_rows):
    grown_cols = cols_dev + 2 * RADIUS
    grown_rows = rows_dev + 2 * RADIUS
    own_ids = jnp.arange(rows_dev * cols_dev)
    own_row = own_ids // cols_dev
    own_col = own_ids % cols_dev
    near_ids = jnp.arange(grown_rows * grown_cols)
    near_row = near_ids // grown_cols
    near_col = near_ids % grown_cols
    close_rows = jnp.abs(near_row[None, :] - RADIUS - own_row[:, None]) <= RADIUS
    close_cols = jnp.abs(near_col[None, :] - RADIUS - own_col[:, None]) <= RADIUS
    global_row = row_start + near_row - RADIUS
    in_grid = (global_row >= 0) & (global_row < grid_rows)
    return close_rows & close_cols & in_grid[None, :]


def shards(inputs, qkv_weight, out_weight, attn_out, log_norm, cotangent):
    rows_dev, cols_dev, model_width = inputs.shape
    tokens_dev = rows_dev * cols_dev
    inner_width = HEADS * HEAD_DIM
    score_scale = HEAD_DIM ** (-0.5)
    grown_rows = rows_dev + 2 * RADIUS
    grown_cols = cols_dev + 2 * RADIUS
    grown_tokens = grown_rows * grown_cols
    grid_tokens = tokens_dev * lax.axis_size("rows") * lax.axis_size("cols")
    grad_factor = grid_tokens ** (-0.5)
    flat_in = inputs.reshape(tokens_dev, model_width)
    flat_cot = cotangent.reshape(tokens_dev, model_width)
    flat_att = attn_out.reshape(tokens_dev, inner_width)
    projected = jnp.dot(flat_in, qkv_weight, preferred_element_type=jnp.float32).astype(
        jnp.bfloat16
    )
    grad_att = lax.dot_general(
        flat_cot, out_weight, (((1,), (1,)), ((), ())), preferred_element_type=jnp.float32
    ).astype(jnp.bfloat16)
    grad_wout = lax.dot_general(
        flat_cot, flat_att, (((0,), (0,)), ((), ())), preferred_element_type=jnp.float32
    )
    head_shape = (tokens_dev, HEADS, HEAD_DIM)
    queries = projected[:, :inner_width].reshape(head_shape)
    own_keyval = projected[:, inner_width:]
    upstream = grad_att.reshape(head_shape)
    row_delta = jnp.sum(
        upstream.astype(jnp.float32) * flat_att.reshape(head_shape).astype(jnp.float32), axis=2
    ).T
    own_norm = log_norm.reshape(HEADS, tokens_dev)
    inside = window_mask(
        rows_dev, cols_dev, lax.axis_index("rows") * rows_dev, rows_dev * lax.axis_size("rows")
    )
    block_keyval = own_keyval.reshape(rows_dev, cols_dev, 2 * inner_width)
    query_side = jnp.concatenate([projected[:, :inner_width], grad_att], axis=1).reshape(
        rows_dev, cols_dev, 2 * inner_width
    )
    near_keyval, near_qdo = (
        padded(block_keyval, (("rows", 0), ("cols", 1)), RADIUS),
        padded(query_side, (("rows", 0), ("cols", 1)), RADIUS),
    )
    own_stats = jnp.concatenate([own_norm, row_delta], axis=0).T.reshape(
        rows_dev, cols_dev, 2 * HEADS
    )
    near_stats = padded(own_stats, (("rows", 0), ("cols", 1)), RADIUS)
    flat_kv = near_keyval.reshape(grown_tokens, 2 * inner_width)
    near_keys = flat_kv[:, :inner_width].reshape(grown_tokens, HEADS, HEAD_DIM)
    near_values = flat_kv[:, inner_width:].reshape(grown_tokens, HEADS, HEAD_DIM)
    scores = (
        jnp.einsum("thd,ehd->hte", queries, near_keys, preferred_element_type=jnp.float32)
        * score_scale
    )
    weight = jnp.where(inside[None], jnp.exp(scores - own_norm[:, :, None]), 0.0)
    grad_weight = jnp.einsum(
        "thd,ehd->hte", upstream, near_values, preferred_element_type=jnp.float32
    )
    grad_score = (weight * (grad_weight - row_delta[:, :, None])).astype(jnp.bfloat16)
    grad_query = (
        jnp.einsum("hte,ehd->thd", grad_score, near_keys, preferred_element_type=jnp.float32)
        * score_scale
    )
    near_flat = near_qdo.reshape(grown_tokens, 2 * inner_width)
    near_queries = near_flat[:, :inner_width].reshape(grown_tokens, HEADS, HEAD_DIM)
    near_upstream = near_flat[:, inner_width:].reshape(grown_tokens, HEADS, HEAD_DIM)
    stats_flat = near_stats.reshape(grown_tokens, 2 * HEADS).T
    near_norm = stats_flat[:HEADS]
    near_delta = stats_flat[HEADS:]
    own_keys = own_keyval[:, :inner_width].reshape(head_shape)
    own_values = own_keyval[:, inner_width:].reshape(head_shape)
    scores_back = (
        jnp.einsum("ehd,thd->het", near_queries, own_keys, preferred_element_type=jnp.float32)
        * score_scale
    )
    weight_back = jnp.where(inside.T[None], jnp.exp(scores_back - near_norm[:, :, None]), 0.0)
    grad_back = jnp.einsum(
        "ehd,thd->het", near_upstream, own_values, preferred_element_type=jnp.float32
    )
    score_back_grad = (weight_back * (grad_back - near_delta[:, :, None])).astype(jnp.bfloat16)
    grad_keys = (
        jnp.einsum(
            "het,ehd->thd", score_back_grad, near_queries, preferred_element_type=jnp.float32
        )
        * score_scale
    )
    grad_values = jnp.einsum(
        "het,ehd->thd",
        weight_back.astype(jnp.bfloat16),
        near_upstream,
        preferred_element_type=jnp.float32,
    )
    grad_keyval = jnp.concatenate(
        [grad_keys.reshape(tokens_dev, inner_width), grad_values.reshape(tokens_dev, inner_width)],
        axis=1,
    )
    grad_proj = jnp.concatenate(
        [grad_query.reshape(tokens_dev, inner_width), grad_keyval], axis=1
    ).astype(jnp.bfloat16)
    grad_input = lax.dot_general(
        grad_proj, qkv_weight, (((1,), (1,)), ((), ())), preferred_element_type=jnp.float32
    ).astype(jnp.bfloat16)
    grad_input = grad_input.reshape(rows_dev, cols_dev, model_width)
    grad_wqkv = lax.dot_general(
        flat_in, grad_proj, (((0,), (0,)), ((), ())), preferred_element_type=jnp.float32
    )
    sums = summed(jnp.concatenate([grad_wqkv, grad_wout], axis=1), grad_factor)
    columns = grad_wqkv.shape[1]
    return grad_input, sums[:, :columns], sums[:, columns:].T


def solution(mesh):
    in_specs = (
        P("rows", "cols", None),
        P(),
        P(),
        P("rows", "cols", None),
        P(None, "rows", "cols"),
        P("rows", "cols", None),
    )
    out_specs = (P("rows", "cols", None), P(), P())
    return jax.shard_map(shards, mesh=mesh, in_specs=in_specs, out_specs=out_specs, check_vma=False)
```

```python
import functools

import jax
import jax.numpy as jnp
import numpy as np
from jax import lax
from jax.experimental import pallas as pl
from jax.experimental.pallas import tpu as pltpu
from jax.sharding import PartitionSpec as P

HEADS = 5
HEAD_DIM = 64
RADIUS = 6


MESH = pl.DeviceIdType.MESH


def reduce_kernel(
    planes, depth, width, factor,
    x_ref, o_ref, recv1, sum1, recv2, sum2, recv3,
    s1, r1, s2, r2, s3, r3, zs, zr, ps, pr, cs, cr,
):
    row, col = lax.axis_index("rows"), lax.axis_index("cols")
    core, lane, z = row % 2, (row // 2) % 2, row // 4
    p = lane * width + col
    partner = (row + 1 - 2 * core, col)
    half = x_ref.shape[3] // 2
    lanes = pl.ds(pl.multiple_of(core * half, 128), half)
    others = pl.ds(pl.multiple_of((1 - core) * half, 128), half)

    def plane_peer(k):
        q = (p + k) % planes
        return q, (z * 4 + (q // width) * 2 + core, q % width)

    def z_peer(k):
        q = (z + k) % depth
        return q, (q * 4 + lane * 2 + core, col)

    def send(src, dst, ssem, rsem, device):
        copy = pltpu.make_async_remote_copy(
            src_ref=src, dst_ref=dst, send_sem=ssem, recv_sem=rsem,
            device_id=device, device_id_type=MESH,
        )
        copy.start()
        return copy

    barrier = pltpu.get_barrier_semaphore()
    peers = [partner]
    peers += [plane_peer(k)[1] for k in range(1, planes)]
    peers += [z_peer(k)[1] for k in range(1, depth)]
    for peer in peers:
        pl.semaphore_signal(barrier, inc=1, device_id=peer, device_id_type=MESH)
    pl.semaphore_wait(barrier, len(peers))

    order = list(range(1, planes)) + [0]
    pair, started = {}, []
    for k in order:
        q = (p + k) % planes
        pair[k] = send(x_ref.at[q, :, :, others], recv1.at[k], s1.at[k], r1.at[k], partner)
    across = {}
    for k in order:
        q, device = plane_peer(k)
        pair[k].wait_recv()
        total = x_ref[q, :, :, lanes].astype(jnp.float32) + recv1[k].astype(jnp.float32)
        sum1[k] = total.astype(jnp.bfloat16)
        if k:
            across[k] = send(sum1.at[k], recv2.at[k - 1], s2.at[k - 1], r2.at[k - 1], device)
    total = sum1[0].astype(jnp.float32)
    for k in range(1, planes):
        across[k].wait_recv()
        total = total + recv2[k - 1].astype(jnp.float32)
    sum2[...] = total.astype(jnp.bfloat16)
    deep = {}
    for k in range(1, depth):
        q, device = z_peer(k)
        deep[k] = send(sum2.at[q], recv3.at[k - 1], s3.at[k - 1], r3.at[k - 1], device)
    total = sum2[z].astype(jnp.float32)
    for k in range(1, depth):
        deep[k].wait_recv()
        total = total + recv3[k - 1].astype(jnp.float32)
    o_ref[p, z, :, lanes] = (total * factor).astype(jnp.bfloat16)

    own = o_ref.at[p, z, :, lanes]
    zcopies, pcopies = {}, {}
    for k in range(1, depth):
        zcopies[k] = send(own, own, zs.at[k - 1], zr.at[k - 1], z_peer(k)[1])

    def share(kz, piece):
        for k in range(1, planes):
            pcopies[k, kz] = send(
                piece, piece, ps.at[k - 1, kz], pr.at[k - 1, kz], plane_peer(k)[1]
            )
        started.append(send(piece, piece, cs.at[0, kz], cr.at[0, kz], partner))

    share(0, own)
    for k in range(1, depth):
        zcopies[k].wait_recv()
        share(k, o_ref.at[p, (z - k + depth) % depth, :, lanes])
    for kz in range(depth):
        for k in range(1, planes):
            pcopies[k, kz].wait_recv()
            piece = o_ref.at[(p - k + planes) % planes, (z - kz + depth) % depth, :, lanes]
            started.append(send(piece, piece, cs.at[k, kz], cr.at[k, kz], partner))
    for copy in started:
        copy.wait_recv()
    for copy in [*started, *pair.values(), *across.values(), *deep.values(),
                 *zcopies.values(), *pcopies.values()]:
        copy.wait_send()


def summed(parts, factor):
    rows = parts.shape[0]
    columns = parts.shape[1]
    count, width = lax.axis_size("rows"), lax.axis_size("cols")
    planes, depth = 2 * width, max(count // 4, 1)
    half = columns // 2
    if count % 4 or rows % (planes * depth * 8) or columns % 256 or depth < 2:
        return (lax.psum(parts.astype(jnp.float32), ("rows", "cols")) * factor).astype(jnp.bfloat16)
    high = rows // (planes * depth)
    x = parts.astype(jnp.bfloat16).reshape(planes, depth, high, columns)
    low = jnp.bfloat16
    dma = pltpu.SemaphoreType.DMA
    out = pl.pallas_call(
        functools.partial(reduce_kernel, planes, depth, width, factor),
        out_shape=jax.ShapeDtypeStruct((planes, depth, high, columns), low),
        in_specs=[pl.BlockSpec(memory_space=pltpu.VMEM)],
        out_specs=pl.BlockSpec(memory_space=pltpu.VMEM),
        scratch_shapes=[
            pltpu.VMEM((planes, depth, high, half), low),
            pltpu.VMEM((planes, depth, high, half), low),
            pltpu.VMEM((planes - 1, depth, high, half), low),
            pltpu.VMEM((depth, high, half), low),
            pltpu.VMEM((depth - 1, high, half), low),
            dma((planes,)), dma((planes,)),
            dma((planes - 1,)), dma((planes - 1,)),
            dma((depth - 1,)), dma((depth - 1,)),
            dma((depth - 1,)), dma((depth - 1,)),
            dma((planes - 1, depth)), dma((planes - 1, depth)),
            dma((planes, depth)), dma((planes, depth)),
        ],
        compiler_params=pltpu.CompilerParams(collective_id=0, has_side_effects=True),
        name="weight_sums",
    )(x)
    return out.reshape(rows, columns)


def padded(block, sides, width):
    for axis, dim in sides:
        count = lax.axis_size(axis)
        forward = [(i, i + 1) for i in range(count - 1)]
        forward.append((count - 1, 0))
        backward = [(target, source) for source, target in forward]
        low = lax.ppermute(
            lax.slice_in_dim(block, block.shape[dim] - width, None, axis=dim), axis, forward
        )
        high = lax.ppermute(lax.slice_in_dim(block, 0, width, axis=dim), axis, backward)
        block = jnp.concatenate([low, block, high], axis=dim)
    return block


def window_mask(rows_dev, cols_dev, row_start, grid_rows):
    grown_cols = cols_dev + 2 * RADIUS
    grown_rows = rows_dev + 2 * RADIUS
    own_ids = jnp.arange(rows_dev * cols_dev)
    own_row = own_ids // cols_dev
    own_col = own_ids % cols_dev
    near_ids = jnp.arange(grown_rows * grown_cols)
    near_row = near_ids // grown_cols
    near_col = near_ids % grown_cols
    close_rows = jnp.abs(near_row[None, :] - RADIUS - own_row[:, None]) <= RADIUS
    close_cols = jnp.abs(near_col[None, :] - RADIUS - own_col[:, None]) <= RADIUS
    global_row = row_start + near_row - RADIUS
    in_grid = (global_row >= 0) & (global_row < grid_rows)
    return close_rows & close_cols & in_grid[None, :]


def shards(inputs, qkv_weight, out_weight, attn_out, log_norm, cotangent):
    rows_dev, cols_dev, model_width = inputs.shape
    tokens_dev = rows_dev * cols_dev
    inner_width = HEADS * HEAD_DIM
    score_scale = HEAD_DIM ** (-0.5)
    grown_rows = rows_dev + 2 * RADIUS
    grown_cols = cols_dev + 2 * RADIUS
    grown_tokens = grown_rows * grown_cols
    grid_tokens = tokens_dev * lax.axis_size("rows") * lax.axis_size("cols")
    grad_factor = grid_tokens ** (-0.5)
    flat_in = inputs.reshape(tokens_dev, model_width)
    flat_cot = cotangent.reshape(tokens_dev, model_width)
    flat_att = attn_out.reshape(tokens_dev, inner_width)
    projected = jnp.dot(flat_in, qkv_weight, preferred_element_type=jnp.float32).astype(
        jnp.bfloat16
    )
    grad_att = lax.dot_general(
        flat_cot, out_weight, (((1,), (1,)), ((), ())), preferred_element_type=jnp.float32
    ).astype(jnp.bfloat16)
    grad_wout = lax.dot_general(
        flat_cot, flat_att, (((0,), (0,)), ((), ())), preferred_element_type=jnp.float32
    )
    head_shape = (tokens_dev, HEADS, HEAD_DIM)
    queries = projected[:, :inner_width].reshape(head_shape)
    own_keyval = projected[:, inner_width:]
    upstream = grad_att.reshape(head_shape)
    row_delta = jnp.sum(
        upstream.astype(jnp.float32) * flat_att.reshape(head_shape).astype(jnp.float32), axis=2
    ).T
    own_norm = log_norm.reshape(HEADS, tokens_dev)
    inside = window_mask(
        rows_dev, cols_dev, lax.axis_index("rows") * rows_dev, rows_dev * lax.axis_size("rows")
    )
    block_keyval = own_keyval.reshape(rows_dev, cols_dev, 2 * inner_width)
    query_side = jnp.concatenate([projected[:, :inner_width], grad_att], axis=1).reshape(
        rows_dev, cols_dev, 2 * inner_width
    )
    near_keyval, near_qdo = (
        padded(block_keyval, (("rows", 0), ("cols", 1)), RADIUS),
        padded(query_side, (("rows", 0), ("cols", 1)), RADIUS),
    )
    own_stats = jnp.concatenate([own_norm, row_delta], axis=0).T.reshape(
        rows_dev, cols_dev, 2 * HEADS
    )
    near_stats = padded(own_stats, (("rows", 0), ("cols", 1)), RADIUS)
    flat_kv = near_keyval.reshape(grown_tokens, 2 * inner_width)
    near_keys = flat_kv[:, :inner_width].reshape(grown_tokens, HEADS, HEAD_DIM)
    near_values = flat_kv[:, inner_width:].reshape(grown_tokens, HEADS, HEAD_DIM)
    scores = (
        jnp.einsum("thd,ehd->hte", queries, near_keys, preferred_element_type=jnp.float32)
        * score_scale
    )
    weight = jnp.where(inside[None], jnp.exp(scores - own_norm[:, :, None]), 0.0)
    grad_weight = jnp.einsum(
        "thd,ehd->hte", upstream, near_values, preferred_element_type=jnp.float32
    )
    grad_score = (weight * (grad_weight - row_delta[:, :, None])).astype(jnp.bfloat16)
    grad_query = (
        jnp.einsum("hte,ehd->thd", grad_score, near_keys, preferred_element_type=jnp.float32)
        * score_scale
    )
    near_flat = near_qdo.reshape(grown_tokens, 2 * inner_width)
    near_queries = near_flat[:, :inner_width].reshape(grown_tokens, HEADS, HEAD_DIM)
    near_upstream = near_flat[:, inner_width:].reshape(grown_tokens, HEADS, HEAD_DIM)
    stats_flat = near_stats.reshape(grown_tokens, 2 * HEADS).T
    near_norm = stats_flat[:HEADS]
    near_delta = stats_flat[HEADS:]
    own_keys = own_keyval[:, :inner_width].reshape(head_shape)
    own_values = own_keyval[:, inner_width:].reshape(head_shape)
    scores_back = (
        jnp.einsum("ehd,thd->het", near_queries, own_keys, preferred_element_type=jnp.float32)
        * score_scale
    )
    weight_back = jnp.where(inside.T[None], jnp.exp(scores_back - near_norm[:, :, None]), 0.0)
    grad_back = jnp.einsum(
        "ehd,thd->het", near_upstream, own_values, preferred_element_type=jnp.float32
    )
    score_back_grad = (weight_back * (grad_back - near_delta[:, :, None])).astype(jnp.bfloat16)
    grad_keys = (
        jnp.einsum(
            "het,ehd->thd", score_back_grad, near_queries, preferred_element_type=jnp.float32
        )
        * score_scale
    )
    grad_values = jnp.einsum(
        "het,ehd->thd",
        weight_back.astype(jnp.bfloat16),
        near_upstream,
        preferred_element_type=jnp.float32,
    )
    grad_keyval = jnp.concatenate(
        [grad_keys.reshape(tokens_dev, inner_width), grad_values.reshape(tokens_dev, inner_width)],
        axis=1,
    )
    grad_proj = jnp.concatenate(
        [grad_query.reshape(tokens_dev, inner_width), grad_keyval], axis=1
    ).astype(jnp.bfloat16)
    grad_input = lax.dot_general(
        grad_proj, qkv_weight, (((1,), (1,)), ((), ())), preferred_element_type=jnp.float32
    ).astype(jnp.bfloat16)
    grad_input = grad_input.reshape(rows_dev, cols_dev, model_width)
    grad_wqkv = lax.dot_general(
        flat_in, grad_proj, (((0,), (0,)), ((), ())), preferred_element_type=jnp.float32
    )
    sums = summed(jnp.concatenate([grad_wqkv, grad_wout], axis=1), grad_factor)
    columns = grad_wqkv.shape[1]
    return grad_input, sums[:, :columns], sums[:, columns:].T


STATS = 128
NT = (((1,), (1,)), ((), ()))
NN = (((1,), (0,)), ((), ()))
TN = (((0,), (0,)), ((), ()))


def dot(a, b, dims=NN):
    return lax.dot_general(a, b, dims, preferred_element_type=jnp.float32)


def terms(x):
    high = x.astype(jnp.bfloat16).astype(jnp.float32)
    return high, (x - high).astype(jnp.bfloat16).astype(jnp.float32)


def project_kernel(in_ref, wqkv_ref, cot_ref, wout_ref, att_ref, norm_ref, perm_ref, o_ref):
    tokens, inner = att_ref.shape
    low = jnp.bfloat16
    perm = perm_ref[...]
    projected = dot(in_ref[...], wqkv_ref[...]).astype(low)
    upstream = dot(cot_ref[...], wout_ref[...], NT).astype(low)
    width = 3 * inner
    product = upstream.astype(jnp.float32) * att_ref[...].astype(jnp.float32)
    lane = lax.broadcasted_iota(jnp.int32, (tokens, STATS), 1)
    stats = jnp.zeros((tokens, STATS), jnp.float32)
    norm = norm_ref[...]
    norm_high, norm_low = terms(norm)
    norm_high, norm_low = dot(perm, norm_high.astype(low), NT), dot(perm, norm_low.astype(low), NT)
    for h in range(HEADS):
        delta = jnp.sum(product[:, h * HEAD_DIM:(h + 1) * HEAD_DIM], axis=1, keepdims=True)
        high, rest = terms(delta)
        stats = jnp.where(lane == 2 * HEADS + h, high, stats)
        stats = jnp.where(lane == 3 * HEADS + h, rest, stats)
    moved = dot(perm, stats.astype(low))
    for h in range(HEADS):
        moved = jnp.where(lane == h, norm_high[:, h:h + 1], moved)
        moved = jnp.where(lane == HEADS + h, norm_low[:, h:h + 1], moved)
    rows = jnp.concatenate([projected, upstream], axis=1)
    o_ref[:, :width + inner] = dot(perm, rows).astype(low)
    o_ref[:, width + inner:] = moved.astype(low)


def halo_kernel(rows_count, edge, x_ref, o_ref, own_sem, rs, rr, xs, xr):
    row, col = lax.axis_index("rows"), lax.axis_index("cols")
    tokens = x_ref.shape[0]
    above = ((row + rows_count - 1) % rows_count, col)
    below = ((row + 1) % rows_count, col)
    beside = (row, 1 - col)

    def send(src, dst, ssem, rsem, device):
        copy = pltpu.make_async_remote_copy(
            src_ref=src, dst_ref=dst, send_sem=ssem, recv_sem=rsem,
            device_id=device, device_id_type=MESH,
        )
        copy.start()
        return copy

    barrier = pltpu.get_barrier_semaphore()
    for peer in (above, below, beside):
        pl.semaphore_signal(barrier, inc=1, device_id=peer, device_id_type=MESH)
    pl.semaphore_wait(barrier, 3)

    def band(slot, first, size):
        return o_ref.at[pl.ds(slot * tokens + first, size), :]

    def side(slot):
        return o_ref.at[pl.ds(3 * tokens + slot * edge, edge), :]

    rest = tokens - edge
    head, tail = x_ref.at[pl.ds(0, edge), :], x_ref.at[pl.ds(edge, rest), :]
    first = {}
    for slot, device in ((2, above), (0, below)):
        first[slot] = send(head, band(slot, 0, edge), rs.at[slot, 0], rr.at[slot, 0], device)
    copies = [send(head, side(1), xs.at[1], xr.at[1], beside)]
    for slot, device in ((2, above), (0, below)):
        copies.append(
            send(tail, band(slot, edge, rest), rs.at[slot, 1], rr.at[slot, 1], device)
        )
    own = pltpu.make_async_copy(x_ref, band(1, 0, tokens), own_sem)
    own.start()
    for slot in (0, 2):
        first[slot].wait_recv()
        copies.append(send(band(slot, 0, edge), side(slot), xs.at[slot], xr.at[slot], beside))
    for copy in copies:
        copy.wait_recv()
    for copy in [*copies, *first.values()]:
        copy.wait_send()
    own.wait()


def attention_kernel(
    near_ref, mask_ref, perm_ref, in_ref, cot_ref, att_ref, wqkv_ref, gin_ref, part_ref, grads,
):
    tokens, inner = att_ref.shape
    low = jnp.bfloat16
    scale = HEAD_DIM ** (-0.5)
    inside = mask_ref[...] > 0.5
    own = pl.ds(tokens, tokens)
    width = 4 * inner
    near_stats = near_ref[:, width:]
    own_stats = near_ref[own, width:].astype(jnp.float32)
    pick_row = lax.broadcasted_iota(jnp.int32, (16, STATS), 0)
    pick_lane = lax.broadcasted_iota(jnp.int32, (16, STATS), 1)
    norm_pick = (pick_row < HEADS) & ((pick_lane == pick_row) | (pick_lane == pick_row + HEADS))
    delta_pick = (pick_row >= HEADS) & (pick_row < 2 * HEADS) & (
        (pick_lane == pick_row + HEADS) | (pick_lane == pick_row + 2 * HEADS)
    )
    pick = jnp.where(norm_pick | delta_pick, 1.0, 0.0).astype(low)
    near_rows = dot(pick, near_stats, NT)
    for h in range(HEADS):
        def part(block, of):
            return near_ref[of, block * inner + h * HEAD_DIM:block * inner + (h + 1) * HEAD_DIM]

        every = slice(None)
        query, key, value, up = (part(b, own) for b in range(4))
        near_query, near_key, near_value, near_up = (part(b, every) for b in range(4))
        norm = own_stats[:, h:h + 1] + own_stats[:, HEADS + h:HEADS + h + 1]
        delta = (
            own_stats[:, 2 * HEADS + h:2 * HEADS + h + 1]
            + own_stats[:, 3 * HEADS + h:3 * HEADS + h + 1]
        )
        scores = dot(query, near_key, NT) * scale
        weight = jnp.where(inside, jnp.exp(scores - norm), 0.0)
        score_grad = (weight * (dot(up, near_value, NT) - delta)).astype(low)
        grad_query = dot(score_grad, near_key) * scale
        near_norm, near_delta = near_rows[h:h + 1], near_rows[HEADS + h:HEADS + h + 1]
        scores = dot(key, near_query, NT) * scale
        weight = jnp.where(inside, jnp.exp(scores - near_norm), 0.0)
        score_grad = (weight * (dot(value, near_up, NT) - near_delta)).astype(low)
        grad_key = dot(score_grad, near_query) * scale
        grad_value = dot(weight.astype(low), near_up)
        for block, grad in enumerate((grad_query, grad_key, grad_value)):
            at = block * inner + h * HEAD_DIM
            grads[:, at:at + HEAD_DIM] = grad.astype(low)
    grad_proj = dot(perm_ref[...], grads[...], TN).astype(low)
    gin_ref[...] = dot(grad_proj, wqkv_ref[...], NT).astype(low)
    part_ref[:, :3 * inner] = dot(in_ref[...], grad_proj, TN).astype(low)
    part_ref[:, 3 * inner:] = dot(cot_ref[...], att_ref[...], TN).astype(low)


def banded(inputs, qkv_weight, out_weight, attn_out, log_norm, cotangent):
    rows_dev, cols_dev, model_width = inputs.shape
    tokens = rows_dev * cols_dev
    inner = HEADS * HEAD_DIM
    rows_count = lax.axis_size("rows")
    grid_rows = rows_count * rows_dev
    edge = -(-2 * RADIUS * rows_dev // 16) * 16
    near = 3 * (tokens + edge)
    low = jnp.bfloat16
    flat_in = inputs.reshape(tokens, model_width)
    flat_cot = cotangent.reshape(tokens, model_width)
    flat_att = attn_out.reshape(tokens, inner)
    cells = [(r, c) for r in range(rows_dev) for c in range(cols_dev)]
    outer = [(r, c) for r, c in cells if c < RADIUS or c >= cols_dev - RADIUS]
    order = outer + [(r, c) for r, c in cells if RADIUS <= c < cols_dev - RADIUS]
    own_row = np.array([r for r, c in order])
    own_col = np.array([c for r, c in order])
    perm = np.zeros((tokens, tokens), np.float32)
    perm[np.arange(tokens), own_row * cols_dev + own_col] = 1.0
    shifts = [-rows_dev, 0, rows_dev]
    beside = np.where(own_col < cols_dev // 2, own_col + cols_dev, own_col - cols_dev)
    near_row = np.concatenate([own_row + d for d in shifts] + [own_row[:edge] + d for d in shifts])
    near_col = np.concatenate([own_col] * 3 + [beside[:edge]] * 3)
    close = (np.abs(near_row[None] - own_row[:, None]) <= RADIUS) & (
        np.abs(near_col[None] - own_col[:, None]) <= RADIUS
    )
    held = lax.axis_index("rows") * rows_dev + jnp.asarray(near_row, jnp.int32)
    in_grid = ((held >= 0) & (held < grid_rows))[None, :]
    mask = jnp.where(in_grid, jnp.asarray(close, jnp.float32), 0.0)
    perm = jnp.asarray(perm, low)
    payload_width = 4 * inner + STATS
    vmem = pl.BlockSpec(memory_space=pltpu.VMEM)
    payload = pl.pallas_call(
        project_kernel,
        out_shape=jax.ShapeDtypeStruct((tokens, payload_width), low),
        in_specs=[vmem] * 7, out_specs=vmem, name="project",
    )(flat_in, qkv_weight, flat_cot, out_weight, flat_att, log_norm.reshape(HEADS, tokens), perm)
    dma = pltpu.SemaphoreType.DMA
    around = pl.pallas_call(
        functools.partial(halo_kernel, rows_count, edge),
        out_shape=jax.ShapeDtypeStruct((near, payload_width), low),
        in_specs=[vmem], out_specs=vmem, name="halo",
        scratch_shapes=[dma, dma((3, 2)), dma((3, 2)), dma((3,)), dma((3,))],
        compiler_params=pltpu.CompilerParams(collective_id=1, has_side_effects=True),
    )(payload)
    grad_input, partial = pl.pallas_call(
        attention_kernel,
        out_shape=(
            jax.ShapeDtypeStruct((tokens, model_width), low),
            jax.ShapeDtypeStruct((model_width, 4 * inner), low),
        ),
        in_specs=[vmem] * 7, out_specs=(vmem, vmem), name="attention",
        scratch_shapes=[pltpu.VMEM((tokens, 3 * inner), low)],
    )(around, mask, perm, flat_in, flat_cot, flat_att, qkv_weight)
    sums = summed(partial, (tokens * rows_count * lax.axis_size("cols")) ** (-0.5))
    return (
        grad_input.reshape(rows_dev, cols_dev, model_width),
        sums[:, :3 * inner],
        sums[:, 3 * inner:].T,
    )


def step(inputs, *rest):
    rows_dev, cols_dev, model_width = inputs.shape
    fits = (
        lax.axis_size("cols") == 2 and lax.axis_size("rows") > 2
        and rows_dev >= RADIUS and cols_dev > 2 * RADIUS and rows_dev * cols_dev % 16 == 0
        and rows_dev * cols_dev <= 256
    )
    return (banded if fits else shards)(inputs, *rest)


def solution(mesh):
    in_specs = (
        P("rows", "cols", None),
        P(),
        P(),
        P("rows", "cols", None),
        P(None, "rows", "cols"),
        P("rows", "cols", None),
    )
    out_specs = (P("rows", "cols", None), P(), P())
    return jax.shard_map(step, mesh=mesh, in_specs=in_specs, out_specs=out_specs, check_vma=False)
```

```python
import functools

import jax
import jax.numpy as jnp
import numpy as np
from jax import lax
from jax.experimental import pallas as pl
from jax.experimental.pallas import tpu as pltpu
from jax.sharding import PartitionSpec as P

HEADS = 5
HEAD_DIM = 64
RADIUS = 6


MESH = pl.DeviceIdType.MESH


def reduce_kernel(
    depth, factor,
    x_ref, o_ref, recv1, sum1, recv2, sum2, recv3,
    s1, r1, s2, r2, s3, r3, zs, zr, ps, pr, cs, cr,
):
    row, col = lax.axis_index("rows"), lax.axis_index("cols")
    core, lane, z = row % 2, (row // 2) % 2, row // 4
    partner = (row + 1 - 2 * core, col)

    def chip(k):
        y = 1 - lane if k >= 2 else lane
        x = 1 - col if k % 2 else col
        return y * 2 + x, (z * 4 + y * 2 + core, x)

    def z_peer(k):
        q = (z + k) % depth
        return q, (q * 4 + lane * 2 + core, col)

    def send(src, dst, ssem, rsem, device):
        copy = pltpu.make_async_remote_copy(
            src_ref=src, dst_ref=dst, send_sem=ssem, recv_sem=rsem,
            device_id=device, device_id_type=MESH,
        )
        copy.start()
        return copy

    barrier = pltpu.get_barrier_semaphore()
    peers = [partner]
    peers += [chip(k)[1] for k in range(1, 4)]
    peers += [z_peer(k)[1] for k in range(1, depth)]
    for peer in peers:
        pl.semaphore_signal(barrier, inc=1, device_id=peer, device_id_type=MESH)
    pl.semaphore_wait(barrier, len(peers))

    copies = []
    pair, across, deep = {}, {}, {}
    z_order = list(range(1, depth)) + [0]
    for k in (3, 1, 2, 0):
        pair[k] = send(
            x_ref.at[1 - core, chip(k)[0]], recv1.at[k], s1.at[k], r1.at[k], partner
        )
    for k in (3, 1, 2, 0):
        q, device = chip(k)
        pair[k].wait_recv()
        total = x_ref[core, q].astype(jnp.float32) + recv1[k].astype(jnp.float32)
        sum1[k] = total.astype(jnp.bfloat16)
        if k:
            for kz in z_order:
                across[k, kz] = send(
                    sum1.at[k, z_peer(kz)[0]], recv2.at[k - 1, kz],
                    s2.at[k - 1, kz], r2.at[k - 1, kz], device,
                )
    for kz in z_order:
        q, device = z_peer(kz)
        total = sum1[0, q].astype(jnp.float32)
        for k in range(1, 4):
            across[k, kz].wait_recv()
            total = total + recv2[k - 1, kz].astype(jnp.float32)
        if kz:
            sum2[kz - 1] = total.astype(jnp.bfloat16)
            deep[kz] = send(
                sum2.at[kz - 1], recv3.at[kz - 1], s3.at[kz - 1], r3.at[kz - 1], device
            )
    for kz in range(1, depth):
        deep[kz].wait_recv()
        total = total + recv3[kz - 1].astype(jnp.float32)
    o_ref[core, chip(0)[0], z] = (total * factor).astype(jnp.bfloat16)

    def piece(k, kz):
        return o_ref.at[core, chip(k)[0], (z - kz + depth) % depth]

    zcopies, pcopies, started = {}, {}, []

    def forward(k, kz):
        started.append(send(piece(k, kz), piece(k, kz), cs.at[k, kz], cr.at[k, kz], partner))

    def share(kz):
        for k in (1, 2):
            pcopies[k, kz] = send(
                piece(0, kz), piece(0, kz), ps.at[k - 1, kz], pr.at[k - 1, kz], chip(k)[1]
            )
        forward(0, kz)

    own = piece(0, 0)
    for k in range(1, depth):
        zcopies[k] = send(own, own, zs.at[k - 1], zr.at[k - 1], z_peer(k)[1])
    share(0)
    for k in range(1, depth):
        zcopies[k].wait_recv()
        share(k)
    for kz in range(depth):
        via = 1 + kz % 2
        for k in (via, 3 - via):
            pcopies[k, kz].wait_recv()
            if k == via:
                pcopies[3, kz] = send(
                    piece(k, kz), piece(k, kz), ps.at[2, kz], pr.at[2, kz], chip(3 - k)[1]
                )
            forward(k, kz)
    for kz in range(depth):
        pcopies[3, kz].wait_recv()
        forward(3, kz)
    for copy in started:
        copy.wait_recv()
    copies = [pair, across, deep, zcopies, pcopies]
    for copy in [c for group in copies for c in group.values()] + started:
        copy.wait_send()


def summed(parts, factor):
    rows, columns = parts.shape
    count, width = lax.axis_size("rows"), lax.axis_size("cols")
    depth = count // 4
    if width != 2 or count % 4 or depth < 2 or rows % (64 * depth) or columns % 128:
        total = lax.psum(parts.astype(jnp.float32), ("rows", "cols"))
        return (total * factor).astype(jnp.bfloat16)
    high = rows // (8 * depth)
    low = jnp.bfloat16
    x = parts.astype(low).reshape(2, 4, depth, high, columns)
    dma = pltpu.SemaphoreType.DMA
    out = pl.pallas_call(
        functools.partial(reduce_kernel, depth, factor),
        out_shape=jax.ShapeDtypeStruct(x.shape, low),
        in_specs=[pl.BlockSpec(memory_space=pltpu.VMEM)],
        out_specs=pl.BlockSpec(memory_space=pltpu.VMEM),
        scratch_shapes=[
            pltpu.VMEM((4, depth, high, columns), low),
            pltpu.VMEM((4, depth, high, columns), low),
            pltpu.VMEM((3, depth, high, columns), low),
            pltpu.VMEM((depth - 1, high, columns), low),
            pltpu.VMEM((depth - 1, high, columns), low),
            dma((4,)), dma((4,)),
            dma((3, depth)), dma((3, depth)),
            dma((depth - 1,)), dma((depth - 1,)),
            dma((depth - 1,)), dma((depth - 1,)),
            dma((3, depth)), dma((3, depth)),
            dma((4, depth)), dma((4, depth)),
        ],
        compiler_params=pltpu.CompilerParams(collective_id=0, has_side_effects=True),
        name="weight_sums",
    )(x)
    return out.reshape(rows, columns)


def padded(block, sides, width):
    for axis, dim in sides:
        count = lax.axis_size(axis)
        forward = [(i, i + 1) for i in range(count - 1)]
        forward.append((count - 1, 0))
        backward = [(target, source) for source, target in forward]
        low = lax.ppermute(
            lax.slice_in_dim(block, block.shape[dim] - width, None, axis=dim), axis, forward
        )
        high = lax.ppermute(lax.slice_in_dim(block, 0, width, axis=dim), axis, backward)
        block = jnp.concatenate([low, block, high], axis=dim)
    return block


def window_mask(rows_dev, cols_dev, row_start, grid_rows):
    grown_cols = cols_dev + 2 * RADIUS
    grown_rows = rows_dev + 2 * RADIUS
    own_ids = jnp.arange(rows_dev * cols_dev)
    own_row = own_ids // cols_dev
    own_col = own_ids % cols_dev
    near_ids = jnp.arange(grown_rows * grown_cols)
    near_row = near_ids // grown_cols
    near_col = near_ids % grown_cols
    close_rows = jnp.abs(near_row[None, :] - RADIUS - own_row[:, None]) <= RADIUS
    close_cols = jnp.abs(near_col[None, :] - RADIUS - own_col[:, None]) <= RADIUS
    global_row = row_start + near_row - RADIUS
    in_grid = (global_row >= 0) & (global_row < grid_rows)
    return close_rows & close_cols & in_grid[None, :]


def shards(inputs, qkv_weight, out_weight, attn_out, log_norm, cotangent):
    rows_dev, cols_dev, model_width = inputs.shape
    tokens_dev = rows_dev * cols_dev
    inner_width = HEADS * HEAD_DIM
    score_scale = HEAD_DIM ** (-0.5)
    grown_rows = rows_dev + 2 * RADIUS
    grown_cols = cols_dev + 2 * RADIUS
    grown_tokens = grown_rows * grown_cols
    grid_tokens = tokens_dev * lax.axis_size("rows") * lax.axis_size("cols")
    grad_factor = grid_tokens ** (-0.5)
    flat_in = inputs.reshape(tokens_dev, model_width)
    flat_cot = cotangent.reshape(tokens_dev, model_width)
    flat_att = attn_out.reshape(tokens_dev, inner_width)
    projected = jnp.dot(flat_in, qkv_weight, preferred_element_type=jnp.float32).astype(
        jnp.bfloat16
    )
    grad_att = lax.dot_general(
        flat_cot, out_weight, (((1,), (1,)), ((), ())), preferred_element_type=jnp.float32
    ).astype(jnp.bfloat16)
    grad_wout = lax.dot_general(
        flat_att, flat_cot, (((0,), (0,)), ((), ())), preferred_element_type=jnp.float32
    )
    head_shape = (tokens_dev, HEADS, HEAD_DIM)
    queries = projected[:, :inner_width].reshape(head_shape)
    own_keyval = projected[:, inner_width:]
    upstream = grad_att.reshape(head_shape)
    row_delta = jnp.sum(
        upstream.astype(jnp.float32) * flat_att.reshape(head_shape).astype(jnp.float32), axis=2
    ).T
    own_norm = log_norm.reshape(HEADS, tokens_dev)
    inside = window_mask(
        rows_dev, cols_dev, lax.axis_index("rows") * rows_dev, rows_dev * lax.axis_size("rows")
    )
    block_keyval = own_keyval.reshape(rows_dev, cols_dev, 2 * inner_width)
    query_side = jnp.concatenate([projected[:, :inner_width], grad_att], axis=1).reshape(
        rows_dev, cols_dev, 2 * inner_width
    )
    near_keyval, near_qdo = (
        padded(block_keyval, (("rows", 0), ("cols", 1)), RADIUS),
        padded(query_side, (("rows", 0), ("cols", 1)), RADIUS),
    )
    own_stats = jnp.concatenate([own_norm, row_delta], axis=0).T.reshape(
        rows_dev, cols_dev, 2 * HEADS
    )
    near_stats = padded(own_stats, (("rows", 0), ("cols", 1)), RADIUS)
    flat_kv = near_keyval.reshape(grown_tokens, 2 * inner_width)
    near_keys = flat_kv[:, :inner_width].reshape(grown_tokens, HEADS, HEAD_DIM)
    near_values = flat_kv[:, inner_width:].reshape(grown_tokens, HEADS, HEAD_DIM)
    scores = (
        jnp.einsum("thd,ehd->hte", queries, near_keys, preferred_element_type=jnp.float32)
        * score_scale
    )
    weight = jnp.where(inside[None], jnp.exp(scores - own_norm[:, :, None]), 0.0)
    grad_weight = jnp.einsum(
        "thd,ehd->hte", upstream, near_values, preferred_element_type=jnp.float32
    )
    grad_score = (weight * (grad_weight - row_delta[:, :, None])).astype(jnp.bfloat16)
    grad_query = (
        jnp.einsum("hte,ehd->thd", grad_score, near_keys, preferred_element_type=jnp.float32)
        * score_scale
    )
    near_flat = near_qdo.reshape(grown_tokens, 2 * inner_width)
    near_queries = near_flat[:, :inner_width].reshape(grown_tokens, HEADS, HEAD_DIM)
    near_upstream = near_flat[:, inner_width:].reshape(grown_tokens, HEADS, HEAD_DIM)
    stats_flat = near_stats.reshape(grown_tokens, 2 * HEADS).T
    near_norm = stats_flat[:HEADS]
    near_delta = stats_flat[HEADS:]
    own_keys = own_keyval[:, :inner_width].reshape(head_shape)
    own_values = own_keyval[:, inner_width:].reshape(head_shape)
    scores_back = (
        jnp.einsum("ehd,thd->het", near_queries, own_keys, preferred_element_type=jnp.float32)
        * score_scale
    )
    weight_back = jnp.where(inside.T[None], jnp.exp(scores_back - near_norm[:, :, None]), 0.0)
    grad_back = jnp.einsum(
        "ehd,thd->het", near_upstream, own_values, preferred_element_type=jnp.float32
    )
    score_back_grad = (weight_back * (grad_back - near_delta[:, :, None])).astype(jnp.bfloat16)
    grad_keys = (
        jnp.einsum(
            "het,ehd->thd", score_back_grad, near_queries, preferred_element_type=jnp.float32
        )
        * score_scale
    )
    grad_values = jnp.einsum(
        "het,ehd->thd",
        weight_back.astype(jnp.bfloat16),
        near_upstream,
        preferred_element_type=jnp.float32,
    )
    grad_keyval = jnp.concatenate(
        [grad_keys.reshape(tokens_dev, inner_width), grad_values.reshape(tokens_dev, inner_width)],
        axis=1,
    )
    grad_proj = jnp.concatenate(
        [grad_query.reshape(tokens_dev, inner_width), grad_keyval], axis=1
    ).astype(jnp.bfloat16)
    grad_input = lax.dot_general(
        grad_proj, qkv_weight, (((1,), (1,)), ((), ())), preferred_element_type=jnp.float32
    ).astype(jnp.bfloat16)
    grad_input = grad_input.reshape(rows_dev, cols_dev, model_width)
    grad_wqkv = lax.dot_general(
        flat_in, grad_proj, (((0,), (0,)), ((), ())), preferred_element_type=jnp.float32
    )
    sums = summed(jnp.concatenate([grad_wqkv.T, grad_wout], axis=0), grad_factor)
    columns = grad_wqkv.shape[1]
    return grad_input, sums[:columns].T, sums[columns:]


STATS = 128
NT = (((1,), (1,)), ((), ()))
NN = (((1,), (0,)), ((), ()))
TN = (((0,), (0,)), ((), ()))


def dot(a, b, dims=NN):
    return lax.dot_general(a, b, dims, preferred_element_type=jnp.float32)


def terms(x):
    high = x.astype(jnp.bfloat16).astype(jnp.float32)
    return high, (x - high).astype(jnp.bfloat16).astype(jnp.float32)


def project_kernel(in_ref, wqkv_ref, cot_ref, wout_ref, att_ref, norm_ref, perm_ref, o_ref):
    tokens, inner = att_ref.shape
    low = jnp.bfloat16
    perm = perm_ref[...]
    projected = dot(in_ref[...], wqkv_ref[...], NT).astype(low)
    upstream = dot(cot_ref[...], wout_ref[...], NT).astype(low)
    width = 3 * inner
    product = upstream.astype(jnp.float32) * att_ref[...].astype(jnp.float32)
    lane = lax.broadcasted_iota(jnp.int32, (tokens, STATS), 1)
    stats = jnp.zeros((tokens, STATS), jnp.float32)
    norm = jnp.concatenate([norm_ref[:, r] for r in range(norm_ref.shape[1])], axis=1)
    norm_high, norm_low = terms(norm)
    norm_high, norm_low = dot(perm, norm_high.astype(low), NT), dot(perm, norm_low.astype(low), NT)
    for h in range(HEADS):
        delta = jnp.sum(product[:, h * HEAD_DIM:(h + 1) * HEAD_DIM], axis=1, keepdims=True)
        high, rest = terms(delta)
        stats = jnp.where(lane == 2 * HEADS + h, high, stats)
        stats = jnp.where(lane == 3 * HEADS + h, rest, stats)
    moved = dot(perm, stats.astype(low))
    for h in range(HEADS):
        moved = jnp.where(lane == h, norm_high[:, h:h + 1], moved)
        moved = jnp.where(lane == HEADS + h, norm_low[:, h:h + 1], moved)
    rows = jnp.concatenate([projected, upstream], axis=1)
    o_ref[:, :width + inner] = dot(perm, rows).astype(low)
    o_ref[:, width + inner:] = moved.astype(low)


def halo_kernel(rows_count, edge, x_ref, o_ref, own_sem, rs, rr, xs, xr):
    row, col = lax.axis_index("rows"), lax.axis_index("cols")
    tokens = x_ref.shape[0]
    above = ((row + rows_count - 1) % rows_count, col)
    below = ((row + 1) % rows_count, col)
    beside = (row, 1 - col)

    def send(src, dst, ssem, rsem, device):
        copy = pltpu.make_async_remote_copy(
            src_ref=src, dst_ref=dst, send_sem=ssem, recv_sem=rsem,
            device_id=device, device_id_type=MESH,
        )
        copy.start()
        return copy

    barrier = pltpu.get_barrier_semaphore()
    for peer in (above, below, beside):
        pl.semaphore_signal(barrier, inc=1, device_id=peer, device_id_type=MESH)
    pl.semaphore_wait(barrier, 3)

    def band(slot, first, size):
        return o_ref.at[pl.ds(slot * tokens + first, size), :]

    def side(slot):
        return o_ref.at[pl.ds(3 * tokens + slot * edge, edge), :]

    rest = tokens - edge
    head, tail = x_ref.at[pl.ds(0, edge), :], x_ref.at[pl.ds(edge, rest), :]
    first = {}
    for slot, device in ((2, above), (0, below)):
        first[slot] = send(head, band(slot, 0, edge), rs.at[slot, 0], rr.at[slot, 0], device)
    copies = [send(head, side(1), xs.at[1], xr.at[1], beside)]
    for slot, device in ((2, above), (0, below)):
        copies.append(
            send(tail, band(slot, edge, rest), rs.at[slot, 1], rr.at[slot, 1], device)
        )
    own = pltpu.make_async_copy(x_ref, band(1, 0, tokens), own_sem)
    own.start()
    for slot in (0, 2):
        first[slot].wait_recv()
        copies.append(send(band(slot, 0, edge), side(slot), xs.at[slot], xr.at[slot], beside))
    for copy in copies:
        copy.wait_recv()
    for copy in [*copies, *first.values()]:
        copy.wait_send()
    own.wait()


def attention_kernel(
    rows_count, near_ref, mask_ref, perm_ref, in_ref, cot_ref, att_ref, wqkv_ref, gin_ref, part_ref, grads,
):
    tokens, inner = att_ref.shape
    low = jnp.bfloat16
    scale = HEAD_DIM ** (-0.5)
    row = lax.axis_index("rows")
    at = lax.broadcasted_iota(jnp.int32, mask_ref.shape, 1)
    edge = mask_ref.shape[1] // 3 - tokens
    above = (at < tokens) | ((at >= 3 * tokens) & (at < 3 * tokens + edge))
    below = ((at >= 2 * tokens) & (at < 3 * tokens)) | (at >= 3 * tokens + 2 * edge)
    outside = (above & (row == 0)) | (below & (row == rows_count - 1))
    inside = (mask_ref[...].astype(jnp.float32) > 0.5) & jnp.logical_not(outside)
    own = pl.ds(tokens, tokens)
    width = 4 * inner
    near_stats = near_ref[:, width:]
    own_stats = near_ref[own, width:].astype(jnp.float32)
    pick_row = lax.broadcasted_iota(jnp.int32, (16, STATS), 0)
    pick_lane = lax.broadcasted_iota(jnp.int32, (16, STATS), 1)
    norm_pick = (pick_row < HEADS) & ((pick_lane == pick_row) | (pick_lane == pick_row + HEADS))
    delta_pick = (pick_row >= HEADS) & (pick_row < 2 * HEADS) & (
        (pick_lane == pick_row + HEADS) | (pick_lane == pick_row + 2 * HEADS)
    )
    pick = jnp.where(norm_pick | delta_pick, 1.0, 0.0).astype(low)
    near_rows = dot(pick, near_stats, NT)
    for h in range(HEADS):
        def part(block, of):
            return near_ref[of, block * inner + h * HEAD_DIM:block * inner + (h + 1) * HEAD_DIM]

        every = slice(None)
        query, key, value, up = (part(b, own) for b in range(4))
        near_query, near_key, near_value, near_up = (part(b, every) for b in range(4))
        norm = own_stats[:, h:h + 1] + own_stats[:, HEADS + h:HEADS + h + 1]
        delta = (
            own_stats[:, 2 * HEADS + h:2 * HEADS + h + 1]
            + own_stats[:, 3 * HEADS + h:3 * HEADS + h + 1]
        )
        scores = dot(query, near_key, NT) * scale
        weight = jnp.where(inside, jnp.exp(scores - norm), 0.0)
        score_grad = (weight * (dot(up, near_value, NT) - delta)).astype(low)
        grad_query = dot(score_grad, near_key) * scale
        near_norm, near_delta = near_rows[h:h + 1], near_rows[HEADS + h:HEADS + h + 1]
        scores = dot(key, near_query, NT) * scale
        weight = jnp.where(inside, jnp.exp(scores - near_norm), 0.0)
        score_grad = (weight * (dot(value, near_up, NT) - near_delta)).astype(low)
        grad_key = dot(score_grad, near_query) * scale
        grad_value = dot(weight.astype(low), near_up)
        for block, grad in enumerate((grad_query, grad_key, grad_value)):
            at = block * inner + h * HEAD_DIM
            grads[:, at:at + HEAD_DIM] = grad.astype(low)
    grad_proj = dot(perm_ref[...], grads[...], TN).astype(low)
    gin_ref[...] = dot(grad_proj, wqkv_ref[...]).astype(low)
    part_ref[:3 * inner] = dot(grad_proj, in_ref[...], TN).astype(low)
    part_ref[3 * inner:] = dot(att_ref[...], cot_ref[...], TN).astype(low)


def banded(inputs, qkv_weight, out_weight, attn_out, log_norm, cotangent):
    rows_dev, cols_dev, model_width = inputs.shape
    tokens = rows_dev * cols_dev
    inner = HEADS * HEAD_DIM
    rows_count = lax.axis_size("rows")
    edge = -(-2 * RADIUS * rows_dev // 16) * 16
    near = 3 * (tokens + edge)
    low = jnp.bfloat16
    flat_in = inputs.reshape(tokens, model_width)
    flat_cot = cotangent.reshape(tokens, model_width)
    flat_att = attn_out.reshape(tokens, inner)
    cells = [(r, c) for r in range(rows_dev) for c in range(cols_dev)]
    outer = [(r, c) for r, c in cells if c < RADIUS or c >= cols_dev - RADIUS]
    order = outer + [(r, c) for r, c in cells if RADIUS <= c < cols_dev - RADIUS]
    own_row = np.array([r for r, c in order])
    own_col = np.array([c for r, c in order])
    perm = np.zeros((tokens, tokens), np.float32)
    perm[np.arange(tokens), own_row * cols_dev + own_col] = 1.0
    shifts = [-rows_dev, 0, rows_dev]
    beside = np.where(own_col < cols_dev // 2, own_col + cols_dev, own_col - cols_dev)
    near_row = np.concatenate([own_row + d for d in shifts] + [own_row[:edge] + d for d in shifts])
    near_col = np.concatenate([own_col] * 3 + [beside[:edge]] * 3)
    close = (np.abs(near_row[None] - own_row[:, None]) <= RADIUS) & (
        np.abs(near_col[None] - own_col[:, None]) <= RADIUS
    )
    mask = jnp.asarray(close, low)
    perm = jnp.asarray(perm, low)
    wqkv = qkv_weight.T
    payload_width = 4 * inner + STATS
    vmem = pl.BlockSpec(memory_space=pltpu.VMEM)
    payload = pl.pallas_call(
        project_kernel,
        out_shape=jax.ShapeDtypeStruct((tokens, payload_width), low),
        in_specs=[vmem] * 7, out_specs=vmem, name="project",
    )(flat_in, wqkv, flat_cot, out_weight, flat_att, log_norm, perm)
    dma = pltpu.SemaphoreType.DMA
    around = pl.pallas_call(
        functools.partial(halo_kernel, rows_count, edge),
        out_shape=jax.ShapeDtypeStruct((near, payload_width), low),
        in_specs=[vmem], out_specs=vmem, name="halo",
        scratch_shapes=[dma, dma((3, 2)), dma((3, 2)), dma((3,)), dma((3,))],
        compiler_params=pltpu.CompilerParams(collective_id=1, has_side_effects=True),
    )(payload)
    grad_input, partial = pl.pallas_call(
        functools.partial(attention_kernel, rows_count),
        out_shape=(
            jax.ShapeDtypeStruct((tokens, model_width), low),
            jax.ShapeDtypeStruct((4 * inner, model_width), low),
        ),
        in_specs=[vmem] * 7, out_specs=(vmem, vmem), name="attention",
        scratch_shapes=[pltpu.VMEM((tokens, 3 * inner), low)],
    )(around, mask, perm, flat_in, flat_cot, flat_att, wqkv)
    sums = summed(partial, (tokens * rows_count * lax.axis_size("cols")) ** (-0.5))
    return (
        grad_input.reshape(rows_dev, cols_dev, model_width),
        sums[:3 * inner].T,
        sums[3 * inner:],
    )


def step(inputs, *rest):
    rows_dev, cols_dev, model_width = inputs.shape
    fits = (
        lax.axis_size("cols") == 2 and lax.axis_size("rows") > 2
        and rows_dev >= RADIUS and cols_dev > 2 * RADIUS and rows_dev * cols_dev % 16 == 0
        and rows_dev * cols_dev <= 256
    )
    return (banded if fits else shards)(inputs, *rest)


def solution(mesh):
    in_specs = (
        P("rows", "cols", None),
        P(),
        P(),
        P("rows", "cols", None),
        P(None, "rows", "cols"),
        P("rows", "cols", None),
    )
    out_specs = (P("rows", "cols", None), P(), P())
    return jax.shard_map(step, mesh=mesh, in_specs=in_specs, out_specs=out_specs, check_vma=False)
```

```python
import functools

import jax
import jax.numpy as jnp
import numpy as np
from jax import lax
from jax.experimental import pallas as pl
from jax.experimental.pallas import tpu as pltpu
from jax.sharding import PartitionSpec as P

HEADS = 5
HEAD_DIM = 64
RADIUS = 6


MESH = pl.DeviceIdType.MESH


def reduce_kernel(
    depth, factor,
    x_ref, o_ref, recv1, sum1, recv2, sum2, recv3,
    s1, r1, s2, r2, s3, r3, zs, zr, ps, pr, cs, cr,
):
    row, col = lax.axis_index("rows"), lax.axis_index("cols")
    core, lane, z = row % 2, (row // 2) % 2, row // 4
    partner = (row + 1 - 2 * core, col)

    def chip(k):
        y = 1 - lane if k >= 2 else lane
        x = 1 - col if k % 2 else col
        return y * 2 + x, (z * 4 + y * 2 + core, x)

    def z_peer(k):
        q = (z + k) % depth
        return q, (q * 4 + lane * 2 + core, col)

    def send(src, dst, ssem, rsem, device):
        copy = pltpu.make_async_remote_copy(
            src_ref=src, dst_ref=dst, send_sem=ssem, recv_sem=rsem,
            device_id=device, device_id_type=MESH,
        )
        copy.start()
        return copy

    barrier = pltpu.get_barrier_semaphore()
    peers = [partner]
    peers += [chip(k)[1] for k in range(1, 4)]
    peers += [z_peer(k)[1] for k in range(1, depth)]
    for peer in peers:
        pl.semaphore_signal(barrier, inc=1, device_id=peer, device_id_type=MESH)
    pl.semaphore_wait(barrier, len(peers))

    copies = []
    pair, across, deep = {}, {}, {}
    z_order = list(range(1, depth)) + [0]
    for k in (3, 1, 2, 0):
        pair[k] = send(
            x_ref.at[1 - core, chip(k)[0]], recv1.at[k], s1.at[k], r1.at[k], partner
        )
    for k in (3, 1, 2, 0):
        q, device = chip(k)
        pair[k].wait_recv()
        total = x_ref[core, q].astype(jnp.float32) + recv1[k].astype(jnp.float32)
        sum1[k] = total.astype(jnp.bfloat16)
        if k:
            for kz in z_order:
                across[k, kz] = send(
                    sum1.at[k, z_peer(kz)[0]], recv2.at[k - 1, kz],
                    s2.at[k - 1, kz], r2.at[k - 1, kz], device,
                )
    for kz in z_order:
        q, device = z_peer(kz)
        total = sum1[0, q].astype(jnp.float32)
        for k in range(1, 4):
            across[k, kz].wait_recv()
            total = total + recv2[k - 1, kz].astype(jnp.float32)
        if kz:
            sum2[kz - 1] = total.astype(jnp.bfloat16)
            deep[kz] = send(
                sum2.at[kz - 1], recv3.at[kz - 1], s3.at[kz - 1], r3.at[kz - 1], device
            )
    for kz in range(1, depth):
        deep[kz].wait_recv()
        total = total + recv3[kz - 1].astype(jnp.float32)
    o_ref[core, chip(0)[0], z] = (total * factor).astype(jnp.bfloat16)

    def piece(k, kz):
        return o_ref.at[core, chip(k)[0], (z - kz + depth) % depth]

    zcopies, pcopies, started = {}, {}, []

    def forward(k, kz):
        started.append(send(piece(k, kz), piece(k, kz), cs.at[k, kz], cr.at[k, kz], partner))

    def share(kz):
        for k in (1, 2):
            pcopies[k, kz] = send(
                piece(0, kz), piece(0, kz), ps.at[k - 1, kz], pr.at[k - 1, kz], chip(k)[1]
            )
        forward(0, kz)

    own = piece(0, 0)
    for k in range(1, depth):
        zcopies[k] = send(own, own, zs.at[k - 1], zr.at[k - 1], z_peer(k)[1])
    share(0)
    for k in range(1, depth):
        zcopies[k].wait_recv()
        share(k)
    for kz in range(depth):
        via = 1 + kz % 2
        for k in (via, 3 - via):
            pcopies[k, kz].wait_recv()
            if k == via:
                pcopies[3, kz] = send(
                    piece(k, kz), piece(k, kz), ps.at[2, kz], pr.at[2, kz], chip(3 - k)[1]
                )
            forward(k, kz)
    for kz in range(depth):
        pcopies[3, kz].wait_recv()
        forward(3, kz)
    for copy in started:
        copy.wait_recv()
    copies = [pair, across, deep, zcopies, pcopies]
    for copy in [c for group in copies for c in group.values()] + started:
        copy.wait_send()


def summed(parts, factor):
    rows, columns = parts.shape
    count, width = lax.axis_size("rows"), lax.axis_size("cols")
    depth = count // 4
    if width != 2 or count % 4 or depth < 2 or rows % (64 * depth) or columns % 128:
        total = lax.psum(parts.astype(jnp.float32), ("rows", "cols"))
        return (total * factor).astype(jnp.bfloat16)
    high = rows // (8 * depth)
    low = jnp.bfloat16
    x = parts.astype(low).reshape(2, 4, depth, high, columns)
    dma = pltpu.SemaphoreType.DMA
    out = pl.pallas_call(
        functools.partial(reduce_kernel, depth, factor),
        out_shape=jax.ShapeDtypeStruct(x.shape, low),
        in_specs=[pl.BlockSpec(memory_space=pltpu.VMEM)],
        out_specs=pl.BlockSpec(memory_space=pltpu.VMEM),
        scratch_shapes=[
            pltpu.VMEM((4, depth, high, columns), low),
            pltpu.VMEM((4, depth, high, columns), low),
            pltpu.VMEM((3, depth, high, columns), low),
            pltpu.VMEM((depth - 1, high, columns), low),
            pltpu.VMEM((depth - 1, high, columns), low),
            dma((4,)), dma((4,)),
            dma((3, depth)), dma((3, depth)),
            dma((depth - 1,)), dma((depth - 1,)),
            dma((depth - 1,)), dma((depth - 1,)),
            dma((3, depth)), dma((3, depth)),
            dma((4, depth)), dma((4, depth)),
        ],
        compiler_params=pltpu.CompilerParams(collective_id=0, has_side_effects=True),
        name="weight_sums",
    )(x)
    return out.reshape(rows, columns)


def padded(block, sides, width):
    for axis, dim in sides:
        count = lax.axis_size(axis)
        forward = [(i, i + 1) for i in range(count - 1)]
        forward.append((count - 1, 0))
        backward = [(target, source) for source, target in forward]
        low = lax.ppermute(
            lax.slice_in_dim(block, block.shape[dim] - width, None, axis=dim), axis, forward
        )
        high = lax.ppermute(lax.slice_in_dim(block, 0, width, axis=dim), axis, backward)
        block = jnp.concatenate([low, block, high], axis=dim)
    return block


def window_mask(rows_dev, cols_dev, row_start, grid_rows):
    grown_cols = cols_dev + 2 * RADIUS
    grown_rows = rows_dev + 2 * RADIUS
    own_ids = jnp.arange(rows_dev * cols_dev)
    own_row = own_ids // cols_dev
    own_col = own_ids % cols_dev
    near_ids = jnp.arange(grown_rows * grown_cols)
    near_row = near_ids // grown_cols
    near_col = near_ids % grown_cols
    close_rows = jnp.abs(near_row[None, :] - RADIUS - own_row[:, None]) <= RADIUS
    close_cols = jnp.abs(near_col[None, :] - RADIUS - own_col[:, None]) <= RADIUS
    global_row = row_start + near_row - RADIUS
    in_grid = (global_row >= 0) & (global_row < grid_rows)
    return close_rows & close_cols & in_grid[None, :]


def shards(inputs, qkv_weight, out_weight, attn_out, log_norm, cotangent):
    rows_dev, cols_dev, model_width = inputs.shape
    tokens_dev = rows_dev * cols_dev
    inner_width = HEADS * HEAD_DIM
    score_scale = HEAD_DIM ** (-0.5)
    grown_rows = rows_dev + 2 * RADIUS
    grown_cols = cols_dev + 2 * RADIUS
    grown_tokens = grown_rows * grown_cols
    grid_tokens = tokens_dev * lax.axis_size("rows") * lax.axis_size("cols")
    grad_factor = grid_tokens ** (-0.5)
    flat_in = inputs.reshape(tokens_dev, model_width)
    flat_cot = cotangent.reshape(tokens_dev, model_width)
    flat_att = attn_out.reshape(tokens_dev, inner_width)
    projected = jnp.dot(flat_in, qkv_weight, preferred_element_type=jnp.float32).astype(
        jnp.bfloat16
    )
    grad_att = lax.dot_general(
        flat_cot, out_weight, (((1,), (1,)), ((), ())), preferred_element_type=jnp.float32
    ).astype(jnp.bfloat16)
    grad_wout = lax.dot_general(
        flat_att, flat_cot, (((0,), (0,)), ((), ())), preferred_element_type=jnp.float32
    )
    head_shape = (tokens_dev, HEADS, HEAD_DIM)
    queries = projected[:, :inner_width].reshape(head_shape)
    own_keyval = projected[:, inner_width:]
    upstream = grad_att.reshape(head_shape)
    row_delta = jnp.sum(
        upstream.astype(jnp.float32) * flat_att.reshape(head_shape).astype(jnp.float32), axis=2
    ).T
    own_norm = log_norm.reshape(HEADS, tokens_dev)
    inside = window_mask(
        rows_dev, cols_dev, lax.axis_index("rows") * rows_dev, rows_dev * lax.axis_size("rows")
    )
    block_keyval = own_keyval.reshape(rows_dev, cols_dev, 2 * inner_width)
    query_side = jnp.concatenate([projected[:, :inner_width], grad_att], axis=1).reshape(
        rows_dev, cols_dev, 2 * inner_width
    )
    near_keyval, near_qdo = (
        padded(block_keyval, (("rows", 0), ("cols", 1)), RADIUS),
        padded(query_side, (("rows", 0), ("cols", 1)), RADIUS),
    )
    own_stats = jnp.concatenate([own_norm, row_delta], axis=0).T.reshape(
        rows_dev, cols_dev, 2 * HEADS
    )
    near_stats = padded(own_stats, (("rows", 0), ("cols", 1)), RADIUS)
    flat_kv = near_keyval.reshape(grown_tokens, 2 * inner_width)
    near_keys = flat_kv[:, :inner_width].reshape(grown_tokens, HEADS, HEAD_DIM)
    near_values = flat_kv[:, inner_width:].reshape(grown_tokens, HEADS, HEAD_DIM)
    scores = (
        jnp.einsum("thd,ehd->hte", queries, near_keys, preferred_element_type=jnp.float32)
        * score_scale
    )
    weight = jnp.where(inside[None], jnp.exp(scores - own_norm[:, :, None]), 0.0)
    grad_weight = jnp.einsum(
        "thd,ehd->hte", upstream, near_values, preferred_element_type=jnp.float32
    )
    grad_score = (weight * (grad_weight - row_delta[:, :, None])).astype(jnp.bfloat16)
    grad_query = (
        jnp.einsum("hte,ehd->thd", grad_score, near_keys, preferred_element_type=jnp.float32)
        * score_scale
    )
    near_flat = near_qdo.reshape(grown_tokens, 2 * inner_width)
    near_queries = near_flat[:, :inner_width].reshape(grown_tokens, HEADS, HEAD_DIM)
    near_upstream = near_flat[:, inner_width:].reshape(grown_tokens, HEADS, HEAD_DIM)
    stats_flat = near_stats.reshape(grown_tokens, 2 * HEADS).T
    near_norm = stats_flat[:HEADS]
    near_delta = stats_flat[HEADS:]
    own_keys = own_keyval[:, :inner_width].reshape(head_shape)
    own_values = own_keyval[:, inner_width:].reshape(head_shape)
    scores_back = (
        jnp.einsum("ehd,thd->het", near_queries, own_keys, preferred_element_type=jnp.float32)
        * score_scale
    )
    weight_back = jnp.where(inside.T[None], jnp.exp(scores_back - near_norm[:, :, None]), 0.0)
    grad_back = jnp.einsum(
        "ehd,thd->het", near_upstream, own_values, preferred_element_type=jnp.float32
    )
    score_back_grad = (weight_back * (grad_back - near_delta[:, :, None])).astype(jnp.bfloat16)
    grad_keys = (
        jnp.einsum(
            "het,ehd->thd", score_back_grad, near_queries, preferred_element_type=jnp.float32
        )
        * score_scale
    )
    grad_values = jnp.einsum(
        "het,ehd->thd",
        weight_back.astype(jnp.bfloat16),
        near_upstream,
        preferred_element_type=jnp.float32,
    )
    grad_keyval = jnp.concatenate(
        [grad_keys.reshape(tokens_dev, inner_width), grad_values.reshape(tokens_dev, inner_width)],
        axis=1,
    )
    grad_proj = jnp.concatenate(
        [grad_query.reshape(tokens_dev, inner_width), grad_keyval], axis=1
    ).astype(jnp.bfloat16)
    grad_input = lax.dot_general(
        grad_proj, qkv_weight, (((1,), (1,)), ((), ())), preferred_element_type=jnp.float32
    ).astype(jnp.bfloat16)
    grad_input = grad_input.reshape(rows_dev, cols_dev, model_width)
    grad_wqkv = lax.dot_general(
        flat_in, grad_proj, (((0,), (0,)), ((), ())), preferred_element_type=jnp.float32
    )
    sums = summed(jnp.concatenate([grad_wqkv.T, grad_wout], axis=0), grad_factor)
    columns = grad_wqkv.shape[1]
    return grad_input, sums[:columns].T, sums[columns:]


STATS = 128
NT = (((1,), (1,)), ((), ()))
NN = (((1,), (0,)), ((), ()))
TN = (((0,), (0,)), ((), ()))


def dot(a, b, dims=NN):
    return lax.dot_general(a, b, dims, preferred_element_type=jnp.float32)


def terms(x):
    high = x.astype(jnp.bfloat16).astype(jnp.float32)
    return high, (x - high).astype(jnp.bfloat16).astype(jnp.float32)


def project_kernel(in_ref, wqkv_ref, cot_ref, wout_ref, att_ref, norm_ref, perm_ref, o_ref):
    tokens, inner = att_ref.shape
    low = jnp.bfloat16
    perm = perm_ref[...]
    projected = dot(in_ref[...], wqkv_ref[...], NT).astype(low)
    upstream = dot(cot_ref[...], wout_ref[...], NT).astype(low)
    width = 3 * inner
    product = upstream.astype(jnp.float32) * att_ref[...].astype(jnp.float32)
    lane = lax.broadcasted_iota(jnp.int32, (tokens, STATS), 1)
    stats = jnp.zeros((tokens, STATS), jnp.float32)
    norm = jnp.concatenate([norm_ref[:, r] for r in range(norm_ref.shape[1])], axis=1)
    norm_high, norm_low = terms(norm)
    norm_high, norm_low = dot(perm, norm_high.astype(low), NT), dot(perm, norm_low.astype(low), NT)
    for h in range(HEADS):
        delta = jnp.sum(product[:, h * HEAD_DIM:(h + 1) * HEAD_DIM], axis=1, keepdims=True)
        high, rest = terms(delta)
        stats = jnp.where(lane == 2 * HEADS + h, high, stats)
        stats = jnp.where(lane == 3 * HEADS + h, rest, stats)
    moved = dot(perm, stats.astype(low))
    for h in range(HEADS):
        moved = jnp.where(lane == h, norm_high[:, h:h + 1], moved)
        moved = jnp.where(lane == HEADS + h, norm_low[:, h:h + 1], moved)
    rows = jnp.concatenate([projected, upstream], axis=1)
    o_ref[:, :width + inner] = dot(perm, rows).astype(low)
    o_ref[:, width + inner:] = moved.astype(low)


def halo_kernel(rows_count, edge, x_ref, o_ref, own_sem, rs, rr):
    row, col = lax.axis_index("rows"), lax.axis_index("cols")
    core = row % 2
    tokens = x_ref.shape[0]
    beside = (row, 1 - col)
    partner = (row + 1 - 2 * core, col)
    far = (row - 1 + 2 * core, col)
    inner_end = (row > 0) & (row < rows_count - 1)
    barrier = pltpu.get_barrier_semaphore()

    def greet(device):
        pl.semaphore_signal(barrier, inc=1, device_id=device, device_id_type=MESH)

    def remote(src, dst, n, device):
        return pltpu.make_async_remote_copy(
            src_ref=src, dst_ref=dst, send_sem=rs.at[n], recv_sem=rr.at[n],
            device_id=device, device_id_type=MESH,
        )

    def band(slot, first, size):
        return o_ref.at[pl.ds(pl.multiple_of(slot * tokens + first, 16), size), :]

    def side(slot):
        return o_ref.at[pl.ds(pl.multiple_of(3 * tokens + slot * edge, 16), edge), :]

    rest = tokens - edge
    head, tail = x_ref.at[pl.ds(0, edge), :], x_ref.at[pl.ds(edge, rest), :]
    far_slot = 2 * core
    near_slot = 2 - far_slot

    @pl.when(inner_end)
    def _():
        greet(far)

    greet(partner)
    greet(beside)
    pl.semaphore_wait(barrier, 2 + inner_end.astype(jnp.int32))

    far_head = remote(head, band(near_slot, 0, edge), 0, far)
    far_tail = remote(tail, band(near_slot, edge, rest), 1, far)
    side_own = remote(head, side(1), 2, beside)
    pair_head = remote(x_ref, band(far_slot, 0, tokens), 3, partner)
    side_far = remote(band(far_slot, 0, edge), side(far_slot), 4, beside)
    side_pair = remote(side(1), side(far_slot), 5, partner)

    @pl.when(inner_end)
    def _():
        far_head.start()

    side_own.start()

    @pl.when(inner_end)
    def _():
        far_tail.start()

    pair_head.start()
    own = pltpu.make_async_copy(x_ref, band(1, 0, tokens), own_sem)
    own.start()

    @pl.when(jnp.logical_not(inner_end))
    def _():
        for view in (band(far_slot, 0, tokens), side(far_slot)):
            view[...] = jnp.zeros(view.shape, view.dtype)

    side_own.wait_recv()
    side_pair.start()

    @pl.when(inner_end)
    def _():
        far_head.wait_recv()
        side_far.start()

    pair_head.wait_recv()
    side_pair.wait_recv()

    @pl.when(inner_end)
    def _():
        far_tail.wait_recv()
        side_far.wait_recv()
        far_head.wait_send()
        far_tail.wait_send()
        side_far.wait_send()

    side_own.wait_send()
    pair_head.wait_send()
    side_pair.wait_send()
    own.wait()


def split_kernel(x_ref, a_ref, b_ref, sems):
    rows = a_ref.shape[0]
    half = rows // 2
    copies = [
        pltpu.make_async_copy(x_ref.at[pl.ds(0, half)], a_ref.at[pl.ds(0, half)], sems.at[0]),
        pltpu.make_async_copy(x_ref.at[pl.ds(half, half)], a_ref.at[pl.ds(half, half)], sems.at[1]),
        pltpu.make_async_copy(x_ref.at[pl.ds(rows, b_ref.shape[0])], b_ref, sems.at[2]),
    ]
    for copy in copies:
        copy.start()
    for copy in copies:
        copy.wait()


def attention_kernel(
    rows_count, near_ref, mask_ref, perm_ref, in_ref, cot_ref, att_ref, wqkv_ref, gin_ref, part_ref, grads,
):
    tokens, inner = att_ref.shape
    low = jnp.bfloat16
    scale = HEAD_DIM ** (-0.5)
    row = lax.axis_index("rows")
    at = lax.broadcasted_iota(jnp.int32, mask_ref.shape, 1)
    edge = mask_ref.shape[1] // 3 - tokens
    above = (at < tokens) | ((at >= 3 * tokens) & (at < 3 * tokens + edge))
    below = ((at >= 2 * tokens) & (at < 3 * tokens)) | (at >= 3 * tokens + 2 * edge)
    outside = (above & (row == 0)) | (below & (row == rows_count - 1))
    inside = (mask_ref[...].astype(jnp.float32) > 0.5) & jnp.logical_not(outside)
    own = pl.ds(tokens, tokens)
    width = 4 * inner
    near_stats = near_ref[:, width:]
    own_stats = near_ref[own, width:].astype(jnp.float32)
    pick_row = lax.broadcasted_iota(jnp.int32, (16, STATS), 0)
    pick_lane = lax.broadcasted_iota(jnp.int32, (16, STATS), 1)
    norm_pick = (pick_row < HEADS) & ((pick_lane == pick_row) | (pick_lane == pick_row + HEADS))
    delta_pick = (pick_row >= HEADS) & (pick_row < 2 * HEADS) & (
        (pick_lane == pick_row + HEADS) | (pick_lane == pick_row + 2 * HEADS)
    )
    pick = jnp.where(norm_pick | delta_pick, 1.0, 0.0).astype(low)
    near_rows = dot(pick, near_stats, NT)
    for h in range(HEADS):
        def part(block, of):
            return near_ref[of, block * inner + h * HEAD_DIM:block * inner + (h + 1) * HEAD_DIM]

        every = slice(None)
        query, key, value, up = (part(b, own) for b in range(4))
        near_query, near_key, near_value, near_up = (part(b, every) for b in range(4))
        norm = own_stats[:, h:h + 1] + own_stats[:, HEADS + h:HEADS + h + 1]
        delta = (
            own_stats[:, 2 * HEADS + h:2 * HEADS + h + 1]
            + own_stats[:, 3 * HEADS + h:3 * HEADS + h + 1]
        )
        scores = dot(query, near_key, NT) * scale
        weight = jnp.where(inside, jnp.exp(scores - norm), 0.0)
        score_grad = (weight * (dot(up, near_value, NT) - delta)).astype(low)
        grad_query = dot(score_grad, near_key) * scale
        near_norm, near_delta = near_rows[h:h + 1], near_rows[HEADS + h:HEADS + h + 1]
        scores = dot(key, near_query, NT) * scale
        weight = jnp.where(inside, jnp.exp(scores - near_norm), 0.0)
        score_grad = (weight * (dot(value, near_up, NT) - near_delta)).astype(low)
        grad_key = dot(score_grad, near_query) * scale
        grad_value = dot(weight.astype(low), near_up)
        for block, grad in enumerate((grad_query, grad_key, grad_value)):
            at = block * inner + h * HEAD_DIM
            grads[:, at:at + HEAD_DIM] = grad.astype(low)
    grad_proj = dot(perm_ref[...], grads[...], TN).astype(low)
    gin_ref[...] = dot(grad_proj, wqkv_ref[...]).astype(low)
    part_ref[:3 * inner] = dot(grad_proj, in_ref[...], TN).astype(low)
    part_ref[3 * inner:] = dot(att_ref[...], cot_ref[...], TN).astype(low)


def banded(inputs, qkv_weight, out_weight, attn_out, log_norm, cotangent):
    rows_dev, cols_dev, model_width = inputs.shape
    tokens = rows_dev * cols_dev
    inner = HEADS * HEAD_DIM
    rows_count = lax.axis_size("rows")
    edge = -(-2 * RADIUS * rows_dev // 16) * 16
    near = 3 * (tokens + edge)
    low = jnp.bfloat16
    flat_in = inputs.reshape(tokens, model_width)
    flat_cot = cotangent.reshape(tokens, model_width)
    flat_att = attn_out.reshape(tokens, inner)
    cells = [(r, c) for r in range(rows_dev) for c in range(cols_dev)]
    outer = [(r, c) for r, c in cells if c < RADIUS or c >= cols_dev - RADIUS]
    order = outer + [(r, c) for r, c in cells if RADIUS <= c < cols_dev - RADIUS]
    own_row = np.array([r for r, c in order])
    own_col = np.array([c for r, c in order])
    perm = np.zeros((tokens, tokens), np.float32)
    perm[np.arange(tokens), own_row * cols_dev + own_col] = 1.0
    shifts = [-rows_dev, 0, rows_dev]
    beside = np.where(own_col < cols_dev // 2, own_col + cols_dev, own_col - cols_dev)
    near_row = np.concatenate([own_row + d for d in shifts] + [own_row[:edge] + d for d in shifts])
    near_col = np.concatenate([own_col] * 3 + [beside[:edge]] * 3)
    close = (np.abs(near_row[None] - own_row[:, None]) <= RADIUS) & (
        np.abs(near_col[None] - own_col[:, None]) <= RADIUS
    )
    mask = jnp.asarray(close, low)
    perm = jnp.asarray(perm, low)
    wqkv = qkv_weight.T
    payload_width = 4 * inner + STATS
    vmem = pl.BlockSpec(memory_space=pltpu.VMEM)
    payload = pl.pallas_call(
        project_kernel,
        out_shape=jax.ShapeDtypeStruct((tokens, payload_width), low),
        in_specs=[vmem] * 7, out_specs=vmem, name="project",
    )(flat_in, wqkv, flat_cot, out_weight, flat_att, log_norm, perm)
    dma = pltpu.SemaphoreType.DMA
    around = pl.pallas_call(
        functools.partial(halo_kernel, rows_count, edge),
        out_shape=jax.ShapeDtypeStruct((near, payload_width), low),
        in_specs=[vmem], out_specs=vmem, name="halo",
        scratch_shapes=[dma, dma((6,)), dma((6,))],
        compiler_params=pltpu.CompilerParams(collective_id=1, has_side_effects=True),
    )(payload)
    grad_input, partial = pl.pallas_call(
        functools.partial(attention_kernel, rows_count),
        out_shape=(
            jax.ShapeDtypeStruct((tokens, model_width), low),
            jax.ShapeDtypeStruct((4 * inner, model_width), low),
        ),
        in_specs=[vmem] * 7, out_specs=(vmem, vmem), name="attention",
        scratch_shapes=[pltpu.VMEM((tokens, 3 * inner), low)],
    )(around, mask, perm, flat_in, flat_cot, flat_att, wqkv)
    sums = summed(partial, (tokens * rows_count * lax.axis_size("cols")) ** (-0.5))
    anywhere = pl.BlockSpec(memory_space=pl.ANY)
    grad_wqkv, grad_wout = pl.pallas_call(
        split_kernel,
        out_shape=(
            jax.ShapeDtypeStruct((3 * inner, model_width), low),
            jax.ShapeDtypeStruct((inner, model_width), low),
        ),
        in_specs=[vmem], out_specs=(anywhere, anywhere), name="split",
        scratch_shapes=[dma((3,))],
    )(sums)
    return (
        grad_input.reshape(rows_dev, cols_dev, model_width),
        grad_wqkv.T,
        grad_wout,
    )


def step(inputs, *rest):
    rows_dev, cols_dev, model_width = inputs.shape
    fits = (
        lax.axis_size("cols") == 2 and lax.axis_size("rows") % 2 == 0
        and rows_dev >= RADIUS and cols_dev > 2 * RADIUS and rows_dev * cols_dev % 16 == 0
        and rows_dev * cols_dev <= 256
    )
    return (banded if fits else shards)(inputs, *rest)


def solution(mesh):
    in_specs = (
        P("rows", "cols", None),
        P(),
        P(),
        P("rows", "cols", None),
        P(None, "rows", "cols"),
        P("rows", "cols", None),
    )
    out_specs = (P("rows", "cols", None), P(), P())
    return jax.shard_map(step, mesh=mesh, in_specs=in_specs, out_specs=out_specs, check_vma=False)
```

```python
import functools

import jax
import jax.numpy as jnp
import numpy as np
from jax import lax
from jax.experimental import pallas as pl
from jax.experimental.pallas import tpu as pltpu
from jax.sharding import PartitionSpec as P

HEADS = 5
HEAD_DIM = 64
RADIUS = 6


MESH = pl.DeviceIdType.MESH


def reduce_kernel(
    depth, factor,
    x_ref, o_ref, recv1, sum1, recv2, sum2, recv3,
    s1, r1, s2, r2, s3, r3, zs, zr, ps, pr, cs, cr,
):
    row, col = lax.axis_index("rows"), lax.axis_index("cols")
    core, lane, z = row % 2, (row // 2) % 2, row // 4
    partner = (row + 1 - 2 * core, col)

    def chip(k):
        y = 1 - lane if k >= 2 else lane
        x = 1 - col if k % 2 else col
        return y * 2 + x, (z * 4 + y * 2 + core, x)

    def z_peer(k):
        q = (z + k) % depth
        return q, (q * 4 + lane * 2 + core, col)

    def send(src, dst, ssem, rsem, device):
        copy = pltpu.make_async_remote_copy(
            src_ref=src, dst_ref=dst, send_sem=ssem, recv_sem=rsem,
            device_id=device, device_id_type=MESH,
        )
        copy.start()
        return copy

    barrier = pltpu.get_barrier_semaphore()
    peers = [partner]
    peers += [chip(k)[1] for k in range(1, 4)]
    peers += [z_peer(k)[1] for k in range(1, depth)]
    for peer in peers:
        pl.semaphore_signal(barrier, inc=1, device_id=peer, device_id_type=MESH)
    pl.semaphore_wait(barrier, len(peers))

    copies = []
    pair, across, deep = {}, {}, {}
    z_order = list(range(1, depth)) + [0]
    for k in (3, 1, 2, 0):
        pair[k] = send(
            x_ref.at[1 - core, chip(k)[0]], recv1.at[k], s1.at[k], r1.at[k], partner
        )
    for k in (3, 1, 2, 0):
        q, device = chip(k)
        pair[k].wait_recv()
        total = x_ref[core, q].astype(jnp.float32) + recv1[k].astype(jnp.float32)
        sum1[k] = total.astype(jnp.bfloat16)
        if k:
            for kz in z_order:
                across[k, kz] = send(
                    sum1.at[k, z_peer(kz)[0]], recv2.at[k - 1, kz],
                    s2.at[k - 1, kz], r2.at[k - 1, kz], device,
                )
    for kz in z_order:
        q, device = z_peer(kz)
        total = sum1[0, q].astype(jnp.float32)
        for k in range(1, 4):
            across[k, kz].wait_recv()
            total = total + recv2[k - 1, kz].astype(jnp.float32)
        if kz:
            sum2[kz - 1] = total.astype(jnp.bfloat16)
            deep[kz] = send(
                sum2.at[kz - 1], recv3.at[kz - 1], s3.at[kz - 1], r3.at[kz - 1], device
            )
    for kz in range(1, depth):
        deep[kz].wait_recv()
        total = total + recv3[kz - 1].astype(jnp.float32)
    o_ref[core, chip(0)[0], z] = (total * factor).astype(jnp.bfloat16)

    def piece(k, kz):
        return o_ref.at[core, chip(k)[0], (z - kz + depth) % depth]

    zcopies, pcopies, started = {}, {}, []

    def forward(k, kz):
        started.append(send(piece(k, kz), piece(k, kz), cs.at[k, kz], cr.at[k, kz], partner))

    def share(kz):
        for k in (1, 2):
            pcopies[k, kz] = send(
                piece(0, kz), piece(0, kz), ps.at[k - 1, kz], pr.at[k - 1, kz], chip(k)[1]
            )
        forward(0, kz)

    own = piece(0, 0)
    for k in range(1, depth):
        zcopies[k] = send(own, own, zs.at[k - 1], zr.at[k - 1], z_peer(k)[1])
    share(0)
    for k in range(1, depth):
        zcopies[k].wait_recv()
        share(k)
    for kz in range(depth):
        via = 1 + kz % 2
        for k in (via, 3 - via):
            pcopies[k, kz].wait_recv()
            if k == via:
                pcopies[3, kz] = send(
                    piece(k, kz), piece(k, kz), ps.at[2, kz], pr.at[2, kz], chip(3 - k)[1]
                )
            forward(k, kz)
    for kz in range(depth):
        pcopies[3, kz].wait_recv()
        forward(3, kz)
    for copy in started:
        copy.wait_recv()
    copies = [pair, across, deep, zcopies, pcopies]
    for copy in [c for group in copies for c in group.values()] + started:
        copy.wait_send()


def summed(parts, factor):
    rows, columns = parts.shape
    count, width = lax.axis_size("rows"), lax.axis_size("cols")
    depth = count // 4
    if width != 2 or count % 4 or depth < 2 or rows % (64 * depth) or columns % 128:
        total = lax.psum(parts.astype(jnp.float32), ("rows", "cols"))
        return (total * factor).astype(jnp.bfloat16)
    high = rows // (8 * depth)
    low = jnp.bfloat16
    x = parts.astype(low).reshape(2, 4, depth, high, columns)
    dma = pltpu.SemaphoreType.DMA
    out = pl.pallas_call(
        functools.partial(reduce_kernel, depth, factor),
        out_shape=jax.ShapeDtypeStruct(x.shape, low),
        in_specs=[pl.BlockSpec(memory_space=pltpu.VMEM)],
        out_specs=pl.BlockSpec(memory_space=pltpu.VMEM),
        scratch_shapes=[
            pltpu.VMEM((4, depth, high, columns), low),
            pltpu.VMEM((4, depth, high, columns), low),
            pltpu.VMEM((3, depth, high, columns), low),
            pltpu.VMEM((depth - 1, high, columns), low),
            pltpu.VMEM((depth - 1, high, columns), low),
            dma((4,)), dma((4,)),
            dma((3, depth)), dma((3, depth)),
            dma((depth - 1,)), dma((depth - 1,)),
            dma((depth - 1,)), dma((depth - 1,)),
            dma((3, depth)), dma((3, depth)),
            dma((4, depth)), dma((4, depth)),
        ],
        compiler_params=pltpu.CompilerParams(collective_id=0, has_side_effects=True, vmem_limit_bytes=GRANT),
        name="weight_sums",
    )(x)
    return out.reshape(rows, columns)


def padded(block, sides, width):
    for axis, dim in sides:
        count = lax.axis_size(axis)
        forward = [(i, i + 1) for i in range(count - 1)]
        forward.append((count - 1, 0))
        backward = [(target, source) for source, target in forward]
        low = lax.ppermute(
            lax.slice_in_dim(block, block.shape[dim] - width, None, axis=dim), axis, forward
        )
        high = lax.ppermute(lax.slice_in_dim(block, 0, width, axis=dim), axis, backward)
        block = jnp.concatenate([low, block, high], axis=dim)
    return block


def window_mask(rows_dev, cols_dev, row_start, grid_rows):
    grown_cols = cols_dev + 2 * RADIUS
    grown_rows = rows_dev + 2 * RADIUS
    own_ids = jnp.arange(rows_dev * cols_dev)
    own_row = own_ids // cols_dev
    own_col = own_ids % cols_dev
    near_ids = jnp.arange(grown_rows * grown_cols)
    near_row = near_ids // grown_cols
    near_col = near_ids % grown_cols
    close_rows = jnp.abs(near_row[None, :] - RADIUS - own_row[:, None]) <= RADIUS
    close_cols = jnp.abs(near_col[None, :] - RADIUS - own_col[:, None]) <= RADIUS
    global_row = row_start + near_row - RADIUS
    in_grid = (global_row >= 0) & (global_row < grid_rows)
    return close_rows & close_cols & in_grid[None, :]


def shards(inputs, qkv_weight, out_weight, attn_out, log_norm, cotangent):
    rows_dev, cols_dev, model_width = inputs.shape
    tokens_dev = rows_dev * cols_dev
    inner_width = HEADS * HEAD_DIM
    score_scale = HEAD_DIM ** (-0.5)
    grown_rows = rows_dev + 2 * RADIUS
    grown_cols = cols_dev + 2 * RADIUS
    grown_tokens = grown_rows * grown_cols
    grid_tokens = tokens_dev * lax.axis_size("rows") * lax.axis_size("cols")
    grad_factor = grid_tokens ** (-0.5)
    flat_in = inputs.reshape(tokens_dev, model_width)
    flat_cot = cotangent.reshape(tokens_dev, model_width)
    flat_att = attn_out.reshape(tokens_dev, inner_width)
    projected = jnp.dot(flat_in, qkv_weight, preferred_element_type=jnp.float32).astype(
        jnp.bfloat16
    )
    grad_att = lax.dot_general(
        flat_cot, out_weight, (((1,), (1,)), ((), ())), preferred_element_type=jnp.float32
    ).astype(jnp.bfloat16)
    grad_wout = lax.dot_general(
        flat_att, flat_cot, (((0,), (0,)), ((), ())), preferred_element_type=jnp.float32
    )
    head_shape = (tokens_dev, HEADS, HEAD_DIM)
    queries = projected[:, :inner_width].reshape(head_shape)
    own_keyval = projected[:, inner_width:]
    upstream = grad_att.reshape(head_shape)
    row_delta = jnp.sum(
        upstream.astype(jnp.float32) * flat_att.reshape(head_shape).astype(jnp.float32), axis=2
    ).T
    own_norm = log_norm.reshape(HEADS, tokens_dev)
    inside = window_mask(
        rows_dev, cols_dev, lax.axis_index("rows") * rows_dev, rows_dev * lax.axis_size("rows")
    )
    block_keyval = own_keyval.reshape(rows_dev, cols_dev, 2 * inner_width)
    query_side = jnp.concatenate([projected[:, :inner_width], grad_att], axis=1).reshape(
        rows_dev, cols_dev, 2 * inner_width
    )
    near_keyval, near_qdo = (
        padded(block_keyval, (("rows", 0), ("cols", 1)), RADIUS),
        padded(query_side, (("rows", 0), ("cols", 1)), RADIUS),
    )
    own_stats = jnp.concatenate([own_norm, row_delta], axis=0).T.reshape(
        rows_dev, cols_dev, 2 * HEADS
    )
    near_stats = padded(own_stats, (("rows", 0), ("cols", 1)), RADIUS)
    flat_kv = near_keyval.reshape(grown_tokens, 2 * inner_width)
    near_keys = flat_kv[:, :inner_width].reshape(grown_tokens, HEADS, HEAD_DIM)
    near_values = flat_kv[:, inner_width:].reshape(grown_tokens, HEADS, HEAD_DIM)
    scores = (
        jnp.einsum("thd,ehd->hte", queries, near_keys, preferred_element_type=jnp.float32)
        * score_scale
    )
    weight = jnp.where(inside[None], jnp.exp(scores - own_norm[:, :, None]), 0.0)
    grad_weight = jnp.einsum(
        "thd,ehd->hte", upstream, near_values, preferred_element_type=jnp.float32
    )
    grad_score = (weight * (grad_weight - row_delta[:, :, None])).astype(jnp.bfloat16)
    grad_query = (
        jnp.einsum("hte,ehd->thd", grad_score, near_keys, preferred_element_type=jnp.float32)
        * score_scale
    )
    near_flat = near_qdo.reshape(grown_tokens, 2 * inner_width)
    near_queries = near_flat[:, :inner_width].reshape(grown_tokens, HEADS, HEAD_DIM)
    near_upstream = near_flat[:, inner_width:].reshape(grown_tokens, HEADS, HEAD_DIM)
    stats_flat = near_stats.reshape(grown_tokens, 2 * HEADS).T
    near_norm = stats_flat[:HEADS]
    near_delta = stats_flat[HEADS:]
    own_keys = own_keyval[:, :inner_width].reshape(head_shape)
    own_values = own_keyval[:, inner_width:].reshape(head_shape)
    scores_back = (
        jnp.einsum("ehd,thd->het", near_queries, own_keys, preferred_element_type=jnp.float32)
        * score_scale
    )
    weight_back = jnp.where(inside.T[None], jnp.exp(scores_back - near_norm[:, :, None]), 0.0)
    grad_back = jnp.einsum(
        "ehd,thd->het", near_upstream, own_values, preferred_element_type=jnp.float32
    )
    score_back_grad = (weight_back * (grad_back - near_delta[:, :, None])).astype(jnp.bfloat16)
    grad_keys = (
        jnp.einsum(
            "het,ehd->thd", score_back_grad, near_queries, preferred_element_type=jnp.float32
        )
        * score_scale
    )
    grad_values = jnp.einsum(
        "het,ehd->thd",
        weight_back.astype(jnp.bfloat16),
        near_upstream,
        preferred_element_type=jnp.float32,
    )
    grad_keyval = jnp.concatenate(
        [grad_keys.reshape(tokens_dev, inner_width), grad_values.reshape(tokens_dev, inner_width)],
        axis=1,
    )
    grad_proj = jnp.concatenate(
        [grad_query.reshape(tokens_dev, inner_width), grad_keyval], axis=1
    ).astype(jnp.bfloat16)
    grad_input = lax.dot_general(
        grad_proj, qkv_weight, (((1,), (1,)), ((), ())), preferred_element_type=jnp.float32
    ).astype(jnp.bfloat16)
    grad_input = grad_input.reshape(rows_dev, cols_dev, model_width)
    grad_wqkv = lax.dot_general(
        flat_in, grad_proj, (((0,), (0,)), ((), ())), preferred_element_type=jnp.float32
    )
    sums = summed(jnp.concatenate([grad_wqkv.T, grad_wout], axis=0), grad_factor)
    columns = grad_wqkv.shape[1]
    return grad_input, sums[:columns].T, sums[columns:]


STATS = 128
GRANT = 32 * 1024 * 1024
NT = (((1,), (1,)), ((), ()))
NN = (((1,), (0,)), ((), ()))
TN = (((0,), (0,)), ((), ()))


def dot(a, b, dims=NN):
    return lax.dot_general(a, b, dims, preferred_element_type=jnp.float32)


def terms(x):
    high = x.astype(jnp.bfloat16).astype(jnp.float32)
    return high, (x - high).astype(jnp.bfloat16).astype(jnp.float32)


def project_kernel(in_ref, wqkv_ref, cot_ref, wout_ref, att_ref, norm_ref, perm_ref, o_ref):
    tokens, inner = att_ref.shape
    low = jnp.bfloat16
    perm = perm_ref[...]
    projected = dot(in_ref[...], wqkv_ref[...], NT).astype(low)
    upstream = dot(cot_ref[...], wout_ref[...], NT).astype(low)
    width = 3 * inner
    product = upstream.astype(jnp.float32) * att_ref[...].astype(jnp.float32)
    lane = lax.broadcasted_iota(jnp.int32, (tokens, STATS), 1)
    stats = jnp.zeros((tokens, STATS), jnp.float32)
    norm = jnp.concatenate([norm_ref[:, r] for r in range(norm_ref.shape[1])], axis=1)
    norm_high, norm_low = terms(norm)
    norm_high, norm_low = dot(perm, norm_high.astype(low), NT), dot(perm, norm_low.astype(low), NT)
    for h in range(HEADS):
        delta = jnp.sum(product[:, h * HEAD_DIM:(h + 1) * HEAD_DIM], axis=1, keepdims=True)
        high, rest = terms(delta)
        stats = jnp.where(lane == 2 * HEADS + h, high, stats)
        stats = jnp.where(lane == 3 * HEADS + h, rest, stats)
    moved = dot(perm, stats.astype(low))
    for h in range(HEADS):
        moved = jnp.where(lane == h, norm_high[:, h:h + 1], moved)
        moved = jnp.where(lane == HEADS + h, norm_low[:, h:h + 1], moved)
    rows = jnp.concatenate([projected, upstream], axis=1)
    o_ref[:, :width + inner] = dot(perm, rows).astype(low)
    o_ref[:, width + inner:] = moved.astype(low)


def halo_kernel(rows_count, edge, x_ref, o_ref, own_sem, rs, rr):
    row, col = lax.axis_index("rows"), lax.axis_index("cols")
    core = row % 2
    tokens = x_ref.shape[0]
    beside = (row, 1 - col)
    partner = (row + 1 - 2 * core, col)
    far = (row - 1 + 2 * core, col)
    inner_end = (row > 0) & (row < rows_count - 1)
    barrier = pltpu.get_barrier_semaphore()

    def greet(device):
        pl.semaphore_signal(barrier, inc=1, device_id=device, device_id_type=MESH)

    def remote(src, dst, n, device):
        return pltpu.make_async_remote_copy(
            src_ref=src, dst_ref=dst, send_sem=rs.at[n], recv_sem=rr.at[n],
            device_id=device, device_id_type=MESH,
        )

    def band(slot, first, size):
        return o_ref.at[pl.ds(pl.multiple_of(slot * tokens + first, 16), size), :]

    def side(slot):
        return o_ref.at[pl.ds(pl.multiple_of(3 * tokens + slot * edge, 16), edge), :]

    rest = tokens - edge
    head, tail = x_ref.at[pl.ds(0, edge), :], x_ref.at[pl.ds(edge, rest), :]
    far_slot = 2 * core
    near_slot = 2 - far_slot

    @pl.when(inner_end)
    def _():
        greet(far)

    greet(partner)
    greet(beside)
    pl.semaphore_wait(barrier, 2 + inner_end.astype(jnp.int32))

    far_head = remote(head, band(near_slot, 0, edge), 0, far)
    far_tail = remote(tail, band(near_slot, edge, rest), 1, far)
    side_own = remote(head, side(1), 2, beside)
    pair_head = remote(x_ref, band(far_slot, 0, tokens), 3, partner)
    side_far = remote(band(far_slot, 0, edge), side(far_slot), 4, beside)
    side_pair = remote(side(1), side(far_slot), 5, partner)

    @pl.when(inner_end)
    def _():
        far_head.start()

    side_own.start()

    @pl.when(inner_end)
    def _():
        far_tail.start()

    pair_head.start()
    own = pltpu.make_async_copy(x_ref, band(1, 0, tokens), own_sem)
    own.start()

    @pl.when(jnp.logical_not(inner_end))
    def _():
        for view in (band(far_slot, 0, tokens), side(far_slot)):
            view[...] = jnp.zeros(view.shape, view.dtype)

    side_own.wait_recv()
    side_pair.start()

    @pl.when(inner_end)
    def _():
        far_head.wait_recv()
        side_far.start()

    pair_head.wait_recv()
    side_pair.wait_recv()

    @pl.when(inner_end)
    def _():
        far_tail.wait_recv()
        side_far.wait_recv()
        far_head.wait_send()
        far_tail.wait_send()
        side_far.wait_send()

    side_own.wait_send()
    pair_head.wait_send()
    side_pair.wait_send()
    own.wait()


def split_kernel(x_ref, a_ref, b_ref, sems):
    rows = a_ref.shape[0]
    half = rows // 2
    copies = [
        pltpu.make_async_copy(x_ref.at[pl.ds(0, half)], a_ref.at[pl.ds(0, half)], sems.at[0]),
        pltpu.make_async_copy(x_ref.at[pl.ds(half, half)], a_ref.at[pl.ds(half, half)], sems.at[1]),
        pltpu.make_async_copy(x_ref.at[pl.ds(rows, b_ref.shape[0])], b_ref, sems.at[2]),
    ]
    for copy in copies:
        copy.start()
    for copy in copies:
        copy.wait()


def attention_kernel(
    rows_count, near_ref, mask_ref, perm_ref, in_ref, cot_ref, att_ref, wqkv_ref, gin_ref, part_ref, grads,
):
    tokens, inner = att_ref.shape
    low = jnp.bfloat16
    scale = HEAD_DIM ** (-0.5)
    row = lax.axis_index("rows")
    at = lax.broadcasted_iota(jnp.int32, mask_ref.shape, 1)
    edge = mask_ref.shape[1] // 3 - tokens
    above = (at < tokens) | ((at >= 3 * tokens) & (at < 3 * tokens + edge))
    below = ((at >= 2 * tokens) & (at < 3 * tokens)) | (at >= 3 * tokens + 2 * edge)
    outside = (above & (row == 0)) | (below & (row == rows_count - 1))
    inside = (mask_ref[...].astype(jnp.float32) > 0.5) & jnp.logical_not(outside)
    own = pl.ds(tokens, tokens)
    width = 4 * inner
    near_stats = near_ref[:, width:]
    own_stats = near_ref[own, width:].astype(jnp.float32)
    pick_row = lax.broadcasted_iota(jnp.int32, (16, STATS), 0)
    pick_lane = lax.broadcasted_iota(jnp.int32, (16, STATS), 1)
    norm_pick = (pick_row < HEADS) & ((pick_lane == pick_row) | (pick_lane == pick_row + HEADS))
    delta_pick = (pick_row >= HEADS) & (pick_row < 2 * HEADS) & (
        (pick_lane == pick_row + HEADS) | (pick_lane == pick_row + 2 * HEADS)
    )
    pick = jnp.where(norm_pick | delta_pick, 1.0, 0.0).astype(low)
    near_rows = dot(pick, near_stats, NT)
    for h in range(HEADS):
        def part(block, of):
            return near_ref[of, block * inner + h * HEAD_DIM:block * inner + (h + 1) * HEAD_DIM]

        every = slice(None)
        query, key, value, up = (part(b, own) for b in range(4))
        near_query, near_key, near_value, near_up = (part(b, every) for b in range(4))
        norm = own_stats[:, h:h + 1] + own_stats[:, HEADS + h:HEADS + h + 1]
        delta = (
            own_stats[:, 2 * HEADS + h:2 * HEADS + h + 1]
            + own_stats[:, 3 * HEADS + h:3 * HEADS + h + 1]
        )
        scores = dot(query, near_key, NT) * scale
        weight = jnp.where(inside, jnp.exp(scores - norm), 0.0)
        score_grad = (weight * (dot(up, near_value, NT) - delta)).astype(low)
        grad_query = dot(score_grad, near_key) * scale
        near_norm, near_delta = near_rows[h:h + 1], near_rows[HEADS + h:HEADS + h + 1]
        scores = dot(key, near_query, NT) * scale
        weight = jnp.where(inside, jnp.exp(scores - near_norm), 0.0)
        score_grad = (weight * (dot(value, near_up, NT) - near_delta)).astype(low)
        grad_key = dot(score_grad, near_query) * scale
        grad_value = dot(weight.astype(low), near_up)
        for block, grad in enumerate((grad_query, grad_key, grad_value)):
            at = block * inner + h * HEAD_DIM
            grads[:, at:at + HEAD_DIM] = grad.astype(low)
    grad_proj = dot(perm_ref[...], grads[...], TN).astype(low)
    gin_ref[...] = dot(grad_proj, wqkv_ref[...]).astype(low)
    part_ref[:3 * inner] = dot(grad_proj, in_ref[...], TN).astype(low)
    part_ref[3 * inner:] = dot(att_ref[...], cot_ref[...], TN).astype(low)


def banded(inputs, qkv_weight, out_weight, attn_out, log_norm, cotangent):
    rows_dev, cols_dev, model_width = inputs.shape
    tokens = rows_dev * cols_dev
    inner = HEADS * HEAD_DIM
    rows_count = lax.axis_size("rows")
    edge = -(-2 * RADIUS * rows_dev // 16) * 16
    near = 3 * (tokens + edge)
    low = jnp.bfloat16
    flat_in = inputs.reshape(tokens, model_width)
    flat_cot = cotangent.reshape(tokens, model_width)
    flat_att = attn_out.reshape(tokens, inner)
    cells = [(r, c) for r in range(rows_dev) for c in range(cols_dev)]
    outer = [(r, c) for r, c in cells if c < RADIUS or c >= cols_dev - RADIUS]
    order = outer + [(r, c) for r, c in cells if RADIUS <= c < cols_dev - RADIUS]
    own_row = np.array([r for r, c in order])
    own_col = np.array([c for r, c in order])
    perm = np.zeros((tokens, tokens), np.float32)
    perm[np.arange(tokens), own_row * cols_dev + own_col] = 1.0
    shifts = [-rows_dev, 0, rows_dev]
    beside = np.where(own_col < cols_dev // 2, own_col + cols_dev, own_col - cols_dev)
    near_row = np.concatenate([own_row + d for d in shifts] + [own_row[:edge] + d for d in shifts])
    near_col = np.concatenate([own_col] * 3 + [beside[:edge]] * 3)
    close = (np.abs(near_row[None] - own_row[:, None]) <= RADIUS) & (
        np.abs(near_col[None] - own_col[:, None]) <= RADIUS
    )
    mask = jnp.asarray(close, low)
    perm = jnp.asarray(perm, low)
    wqkv = qkv_weight.T
    payload_width = 4 * inner + STATS
    vmem = pl.BlockSpec(memory_space=pltpu.VMEM)
    payload = pl.pallas_call(
        project_kernel,
        out_shape=jax.ShapeDtypeStruct((tokens, payload_width), low),
        in_specs=[vmem] * 7, out_specs=vmem, name="project",
        compiler_params=pltpu.CompilerParams(vmem_limit_bytes=GRANT),
    )(flat_in, wqkv, flat_cot, out_weight, flat_att, log_norm, perm)
    dma = pltpu.SemaphoreType.DMA
    around = pl.pallas_call(
        functools.partial(halo_kernel, rows_count, edge),
        out_shape=jax.ShapeDtypeStruct((near, payload_width), low),
        in_specs=[vmem], out_specs=vmem, name="halo",
        scratch_shapes=[dma, dma((6,)), dma((6,))],
        compiler_params=pltpu.CompilerParams(collective_id=1, has_side_effects=True, vmem_limit_bytes=GRANT),
    )(payload)
    grad_input, partial = pl.pallas_call(
        functools.partial(attention_kernel, rows_count),
        out_shape=(
            jax.ShapeDtypeStruct((tokens, model_width), low),
            jax.ShapeDtypeStruct((4 * inner, model_width), low),
        ),
        in_specs=[vmem] * 7, out_specs=(vmem, vmem), name="attention",
        scratch_shapes=[pltpu.VMEM((tokens, 3 * inner), low)],
        compiler_params=pltpu.CompilerParams(vmem_limit_bytes=GRANT),
    )(around, mask, perm, flat_in, flat_cot, flat_att, wqkv)
    sums = summed(partial, (tokens * rows_count * lax.axis_size("cols")) ** (-0.5))
    anywhere = pl.BlockSpec(memory_space=pl.ANY)
    grad_wqkv, grad_wout = pl.pallas_call(
        split_kernel,
        out_shape=(
            jax.ShapeDtypeStruct((3 * inner, model_width), low),
            jax.ShapeDtypeStruct((inner, model_width), low),
        ),
        in_specs=[vmem], out_specs=(anywhere, anywhere), name="split",
        scratch_shapes=[dma((3,))],
        compiler_params=pltpu.CompilerParams(vmem_limit_bytes=GRANT),
    )(sums)
    return (
        grad_input.reshape(rows_dev, cols_dev, model_width),
        grad_wqkv.T,
        grad_wout,
    )


def step(inputs, *rest):
    rows_dev, cols_dev, model_width = inputs.shape
    fits = (
        lax.axis_size("cols") == 2 and lax.axis_size("rows") % 2 == 0
        and rows_dev >= RADIUS and cols_dev > 2 * RADIUS and rows_dev * cols_dev % 16 == 0
        and rows_dev * cols_dev <= 256
    )
    return (banded if fits else shards)(inputs, *rest)


def solution(mesh):
    in_specs = (
        P("rows", "cols", None),
        P(),
        P(),
        P("rows", "cols", None),
        P(None, "rows", "cols"),
        P("rows", "cols", None),
    )
    out_specs = (P("rows", "cols", None), P(), P())
    return jax.shard_map(step, mesh=mesh, in_specs=in_specs, out_specs=out_specs, check_vma=False)
```
